256 devices in a mesh: clus: 16 (over x, y), leaf: 16 (over z, core).
Axes of the slice: x: 4, y: 4, z: 8, core: 2. Of those that a mesh axis runs over, the one named last changes fastest.
Arguments:
- points: bfloat16 [64, 524288], P(None, ('clus', 'leaf')), may hold values from -6 to 6
- weights: bfloat16 [512, 524288], P(None, ('clus', 'leaf')), may hold values from -2 to 2
- targets: bfloat16 [512, 524288], P(None, ('clus', 'leaf')), may hold values from -6 to 6
- near_lists: int32 [1024, 4], P(('clus', 'leaf')), may hold values from 0 to 1023, as said below
- tile_counts: int32 [1024], P(('clus', 'leaf')), may hold values from 2 to 4, as said below
- skeleton: int32 [256, 256], P(('clus', 'leaf')), may hold values from 0 to 2047, as said below
Outputs:
- precond: float32 [512, 524288], P(None, ('clus', 'leaf'))
The draws below stay inside these ranges and needn't reach their ends.
Inputs may be any that keep to these rules, and one draw needn't show every extreme that they name: `near_lists`: row g lists cluster ids; its first entry is g; its first tile_counts[g] entries are distinct, and the rest repeat g. Every listed cluster lies on a device with the same leaf index as cluster g's device and a clus index at most 1 away; some cluster lists one exactly 1 away. `tile_counts`: some cluster has exactly 4 tiles. `skeleton`: each row holds 256 distinct indices of points of its device; their order matters.
All inputs are finite; a program needn't handle non-finite values.
Results may differ from the reference program's by a relative error of at most 0.0039.
Values may be sent and summed in bfloat16 or wider, within the bound.
No kernel may reach another device: no remote copies, remote signals or barrier semaphores. Data moves between devices by JAX's collectives and lax.ppermute only.
A program may use at most 128 MiB of HBM per device.

```python
import jax
import jax.numpy as jnp
from jax import lax

FEATURES = 64
RHS_COLS = 512
CLUSTER_PTS = 512
SKELETON = 256
CLUS_DEV = 4
TILES_MAX = 4
NEAR_REACH = 1
PTS_DEV = 2048
CLUSTERS = 1024
POINTS = 524288
LEVELS = 4
N_CLUS = 16
N_LEAF = 16
DEVICES = 256


def draw_points(key, part):
    base_key = jax.random.fold_in(key, 53)
    sign_key, center_key, latent_key, noise_key = jax.random.split(base_key, 4)
    sign_cols = jnp.where(jax.random.bernoulli(sign_key, 0.5, (FEATURES, 2)), 1.0, -1.0).astype(jnp.float32)
    centers = jax.random.uniform(center_key, (DEVICES, 2), jnp.float32, -0.75, 0.75)
    owner_dev = jnp.arange(POINTS, dtype=jnp.int32) // PTS_DEV
    centre_cols = jnp.take(centers, owner_dev, axis=0)
    latent = jax.random.uniform(latent_key, (POINTS, 2), jnp.float32, -1.0, 1.0)
    noise_part = 0.15 * jax.random.normal(noise_key, (FEATURES, POINTS), jnp.float32)
    coords = centre_cols + latent
    values = (sign_cols[:, 0:1] * coords[None, :, 0] + sign_cols[:, 1:2] * coords[None, :, 1]) * 0.70710678 + noise_part
    return jnp.clip(values, -6.0, 6.0).astype(jnp.bfloat16)


def near_tables(key):
    base_key = jax.random.fold_in(key, 31)
    score_key, count_key = jax.random.split(base_key)
    window_len = 2 * NEAR_REACH + 1
    choices_n = window_len * CLUS_DEV
    cluster_id = jnp.arange(CLUSTERS, dtype=jnp.int32)
    device_id = cluster_id // CLUS_DEV
    clus_idx = device_id // N_LEAF
    leaf_idx = device_id % N_LEAF
    slot_ids = jnp.arange(choices_n, dtype=jnp.int32)
    offsets = slot_ids // CLUS_DEV - NEAR_REACH
    member = slot_ids % CLUS_DEV
    cand_clus = clus_idx[:, None] + offsets[None, :]
    valid_cand = (cand_clus >= 0) & (cand_clus < N_CLUS)
    cand_id = (cand_clus * N_LEAF + leaf_idx[:, None]) * CLUS_DEV + member[None, :]
    own_cand = cand_id == cluster_id[:, None]
    scores = jax.random.randint(score_key, (CLUSTERS, choices_n), 0, 1 << 20, dtype=jnp.int32) * choices_n + slot_ids[None, :] + 1
    forced = (cluster_id[:, None] == 0) & (offsets[None, :] == NEAR_REACH) & (member[None, :] == 0)
    scores = jnp.where(forced, 0, scores)
    scores = jnp.where(own_cand, -1, scores)
    scores = jnp.where(valid_cand, scores, 1 << 30)
    order_idx = jnp.argsort(scores, axis=1, stable=True)
    ranked = jnp.take_along_axis(cand_id, order_idx, axis=1)[:, :TILES_MAX]
    draws_u = jax.random.randint(count_key, (CLUSTERS,), 0, 64, dtype=jnp.int32)
    counts = 2 + draws_u * draws_u * (TILES_MAX - 2) // 3969
    counts = jnp.where(cluster_id == 0, TILES_MAX, counts)
    slot_pos = jnp.arange(TILES_MAX, dtype=jnp.int32)[None, :]
    listed = jnp.where(slot_pos < counts[:, None], ranked, cluster_id[:, None])
    return (listed.astype(jnp.int32), counts.astype(jnp.int32))


def draw_near_lists(key, part):
    return near_tables(key)[0]


def draw_tile_counts(key, part):
    return near_tables(key)[1]


def draw_skeleton(key, part):

    def one_row(row_key):
        first_key, second_key = jax.random.split(row_key)
        inner = (jax.random.permutation(first_key, PTS_DEV - 2) + 1).astype(jnp.int32)
        chosen = jnp.concatenate([jnp.array([0, PTS_DEV - 1], dtype=jnp.int32), inner[:SKELETON - 2]])
        return chosen[jax.random.permutation(second_key, SKELETON)]
    row_keys = jax.random.split(jax.random.fold_in(key, 17), DEVICES)
    return jax.vmap(one_row)(row_keys).astype(jnp.int32)


def level_of(rng, extent, shards, low, top_value):
    def one(dim, blocks):
        heights = jax.random.uniform(jax.random.fold_in(jax.random.fold_in(rng, 6), dim), (blocks,), jnp.float32, low / len(shards), top_value / len(shards))
        return jnp.repeat(jnp.exp(heights), extent[dim] // blocks).reshape((-1,) + (1,) * (len(extent) - dim - 1))

    level = one(*shards[0])
    for cut in shards[1:]:
        level = level * one(*cut)
    return level


def bell_draw(key, dims, scale, most, pieces=(), held_as=jnp.bfloat16):
    values = jax.random.normal(key, dims, jnp.float32) * scale
    if len(pieces) > 0:
        values = level_of(key, dims, pieces, -0.22, 0.18) * values
    return jnp.clip(values, min=-most, max=most).astype(held_as)


def setup_inputs(seed: int = 0) -> dict:
    seeds = jax.random.split(jax.random.key(seed), 7)
    return {
        "points": draw_points(jax.random.fold_in(seeds[6], 71), 0),
        "weights": bell_draw(seeds[1], (RHS_COLS, POINTS), 0.15, 2.0, ((1, 256),)),
        "targets": bell_draw(seeds[2], (RHS_COLS, POINTS), 1.0, 6.0, ((1, 256),)),
        "near_lists": draw_near_lists(jax.random.fold_in(seeds[6], 71), 0),
        "tile_counts": draw_tile_counts(jax.random.fold_in(seeds[6], 71), 0),
        "skeleton": draw_skeleton(jax.random.fold_in(seeds[6], 71), 0),
    }


ridge_term = 0.5
node_shift = 4.0

def kernel_tile(row_pts, col_pts):
    row_pts = row_pts.astype(jnp.float32)
    col_pts = col_pts.astype(jnp.float32)
    cross_dot = lax.dot_general(row_pts.astype(jnp.float32), col_pts.astype(jnp.float32), (((0,), (0,)), ((), ())), precision=lax.Precision.HIGHEST, preferred_element_type=jnp.float32)
    row_sq = jnp.sum(row_pts * row_pts, axis=0)
    col_sq = jnp.sum(col_pts * col_pts, axis=0)
    scale_exp = 2.0 / row_pts.shape[0]
    return jnp.exp(-scale_exp * (row_sq[:, None] + col_sq[None, :] - 2.0 * cross_dot))

def solve_right(factor_low, values):
    partial_sol = lax.linalg.triangular_solve(factor_low, values, left_side=False, lower=True, transpose_a=True)
    return lax.linalg.triangular_solve(factor_low, partial_sol, left_side=False, lower=True, transpose_a=False)

def node_solve(node_pts, node_res):
    gram_mat = kernel_tile(node_pts, node_pts) + node_shift * jnp.eye(node_pts.shape[1], dtype=jnp.float32)
    return solve_right(jnp.linalg.cholesky(gram_mat), node_res)

def tile_term(own_pts, other_pts, other_w):
    tile_low = lax.optimization_barrier(kernel_tile(other_pts, own_pts).astype(jnp.bfloat16))
    return jnp.dot(other_w.astype(jnp.float32), tile_low.astype(jnp.float32), precision=lax.Precision.HIGHEST)

def near_field(points, weights, near_lists, tile_counts):

    def one_cluster(cluster_id):
        own_pts = lax.dynamic_slice_in_dim(points, (cluster_id * CLUSTER_PTS).astype(jnp.int32), CLUSTER_PTS, 1)

        def add_tile(slot_idx, summed):
            listed_id = near_lists[cluster_id, slot_idx]

            def compute():
                begin_col = (listed_id * CLUSTER_PTS).astype(jnp.int32)
                other_pts = lax.dynamic_slice_in_dim(points, begin_col, CLUSTER_PTS, 1)
                other_w = lax.dynamic_slice_in_dim(weights, begin_col, CLUSTER_PTS, 1)
                return tile_term(own_pts, other_pts, other_w)

            def nothing():
                return jnp.zeros((RHS_COLS, CLUSTER_PTS), jnp.float32)
            return summed + lax.cond(slot_idx < tile_counts[cluster_id], compute, nothing)
        return lax.fori_loop(0, TILES_MAX, add_tile, jnp.zeros((RHS_COLS, CLUSTER_PTS), jnp.float32))
    blocks = lax.map(one_cluster, jnp.arange(CLUSTERS, dtype=jnp.int32))
    return jnp.transpose(blocks, (1, 0, 2)).reshape(RHS_COLS, POINTS)

def tree_correction(points, residual, skeleton):
    row_idx = (jnp.arange(DEVICES, dtype=jnp.int32)[:, None] * PTS_DEV + skeleton).astype(jnp.int32)
    node_pts = jnp.transpose(jnp.take(points, row_idx, axis=1), (1, 0, 2))
    node_res = jnp.transpose(jnp.take(residual, row_idx, axis=1), (1, 0, 2))
    base_pts = node_pts
    half_s = SKELETON // 2
    node_pts = node_pts.reshape(N_CLUS, N_LEAF, FEATURES, SKELETON)
    node_res = node_res.reshape(N_CLUS, N_LEAF, RHS_COLS, SKELETON)
    solver = jax.vmap(jax.vmap(node_solve))
    stored = []
    for level_idx in range(LEVELS):
        solved = solver(node_pts, node_res)
        stored.append(solved)
        node_pts = jnp.concatenate([node_pts[:, 0::2, :, :half_s], node_pts[:, 1::2, :, :half_s]], axis=3)
        node_res = node_shift * jnp.concatenate([solved[:, 0::2, :, :half_s], solved[:, 1::2, :, :half_s]], axis=3)
    correction = solver(node_pts, node_res)
    for level_idx in reversed(range(LEVELS)):
        inject = jnp.stack([correction[..., :half_s], correction[..., half_s:]], axis=2)
        inject = inject.reshape(N_CLUS, -1, RHS_COLS, half_s)
        correction = stored[level_idx] + jnp.concatenate([inject, jnp.zeros_like(inject)], axis=3)
    return (base_pts, correction.reshape(DEVICES, RHS_COLS, SKELETON))

def prolong(dev_pts, dev_res, base_pts, correction, skel_row):
    tile_low = lax.optimization_barrier(kernel_tile(base_pts, dev_pts).astype(jnp.bfloat16))
    corr_low = lax.optimization_barrier(correction.astype(jnp.bfloat16))
    spread = jnp.dot(corr_low.astype(jnp.float32), tile_low.astype(jnp.float32), precision=lax.Precision.HIGHEST)
    result = dev_res / (1.0 + ridge_term) + spread
    return result.at[:, skel_row].add(correction)

def reference(points, weights, targets, near_lists, tile_counts, skeleton):
    near_sum = near_field(points, weights, near_lists, tile_counts)
    residual = targets.astype(jnp.float32) - ridge_term * weights.astype(jnp.float32) - near_sum
    base_pts, correction = tree_correction(points, residual, skeleton)

    def per_device(dev_idx):
        begin_col = (dev_idx * PTS_DEV).astype(jnp.int32)
        dev_pts = lax.dynamic_slice_in_dim(points, begin_col, PTS_DEV, 1)
        dev_res = lax.dynamic_slice_in_dim(residual, begin_col, PTS_DEV, 1)
        return prolong(dev_pts, dev_res, base_pts[dev_idx], correction[dev_idx], skeleton[dev_idx])
    blocks = lax.map(per_device, jnp.arange(DEVICES, dtype=jnp.int32))
    return jnp.transpose(blocks, (1, 0, 2)).reshape(RHS_COLS, POINTS)
```

```python
import functools

import jax
import jax.numpy as jnp
from jax import lax
from jax.experimental import pallas as pl
from jax.experimental.pallas import tpu as pltpu
from jax.sharding import PartitionSpec as P


CLUSTER_PTS = 512
RIDGE = 0.5
SHIFT = 4.0
LATE_ROWS = 128
COARSE_STEPS = 4
FINE_STEPS = 2

f32 = jnp.float32
bf16 = jnp.bfloat16
MIB = 1 << 20
VMEM = pl.BlockSpec(memory_space=pltpu.VMEM)
SMEM = pl.BlockSpec(memory_space=pltpu.SMEM)


def mm(a, b):
    return jnp.dot(a, b, preferred_element_type=f32)


def mm_t(a, b):
    return lax.dot_general(a, b, (((1,), (1,)), ((), ())), preferred_element_type=f32)


def split(a):
    high = a.astype(bf16)
    return high, (a - high.astype(f32)).astype(bf16)


def lifted(x):
    wide = x.astype(f32)
    half = -0.5 * jnp.sum(wide * wide, axis=0, keepdims=True)
    high = half.astype(bf16).astype(f32)
    rest = half - high
    mid = rest.astype(bf16).astype(f32)
    low = rest - mid
    row = lax.broadcasted_iota(jnp.int32, (16, x.shape[1]), 0)

    def tail(at, ones):
        out = jnp.where((row >= ones) & (row < ones + 3), 1.0, 0.0)
        out = jnp.where(row == at, high, out)
        out = jnp.where(row == at + 1, mid, out)
        return jnp.where(row == at + 2, low, out).astype(bf16)

    left = jnp.concatenate([x, tail(0, 3)], axis=0)
    right = jnp.concatenate([x, tail(3, 0)], axis=0)
    return left, right


def kernel_of(left, right, features):
    half = lax.dot_general(left, right, (((0,), (0,)), ((), ())), preferred_element_type=f32)
    return jnp.exp((4.0 / features) * half)


def params(mib=24):
    return pltpu.CompilerParams(vmem_limit_bytes=mib * MIB)


def prep_kernel(pts, skel, pick, node_pts, kept):
    n, s = pick.shape
    row = lax.broadcasted_iota(jnp.int32, (n, s), 0)
    chosen = jnp.where(row == skel[...], 1.0, 0.0).astype(bf16)
    pick[...] = chosen
    gathered = mm(pts[...], chosen).astype(bf16)
    node_pts[...] = gathered
    kept[...] = gathered[:, : s // 2]


def prep(points, skeleton):
    features, n = points.shape
    s = skeleton.shape[1]
    return pl.pallas_call(
        prep_kernel,
        out_shape=(
            jax.ShapeDtypeStruct((n, s), bf16),
            jax.ShapeDtypeStruct((features, s), bf16),
            jax.ShapeDtypeStruct((features, s // 2), bf16),
        ),
        in_specs=[VMEM, VMEM],
        out_specs=(VMEM, VMEM, VMEM),
        compiler_params=params(),
        name="prep",
    )(points, skeleton)


def invert(grams):
    s = grams[0].shape[0]
    eye = jnp.where(
        lax.broadcasted_iota(jnp.int32, (s, s), 0) == lax.broadcasted_iota(jnp.int32, (s, s), 1),
        1.0,
        0.0,
    ).astype(f32)
    parts, guesses, gaps = [], [], []
    for gram in grams:
        gram = gram + SHIFT * eye
        top = jnp.max(jnp.sum(gram, axis=0, keepdims=True), axis=1, keepdims=True)
        alpha = 2.0 / (top + SHIFT)
        gap = (top - SHIFT) / (top + SHIFT)
        gain = 2.0 / (2.0 - gap * gap)
        parts.append(split(gram))
        guesses.append((gain * alpha) * (2.0 * eye - alpha * gram))
        gaps.append(0.5 * gain * gap * gap)
    for _ in range(COARSE_STEPS):
        lows = [x.astype(bf16) for x in guesses]
        prods = [mm(gh, x) + mm(gl, x) for (gh, gl), x in zip(parts, lows)]
        gains = [2.0 / (2.0 - gap * gap) for gap in gaps]
        guesses = [
            gain * mm(x, (2.0 * eye - p).astype(bf16)) for gain, x, p in zip(gains, lows, prods)
        ]
        gaps = [0.5 * gain * gap * gap for gain, gap in zip(gains, gaps)]
    for _ in range(FINE_STEPS):
        splits = [split(x) for x in guesses]
        prods = [
            mm(gh, xh) + (mm(gh, xl) + mm(gl, xh)) for (gh, gl), (xh, xl) in zip(parts, splits)
        ]
        guesses = [
            x + mm(xh, (eye - p).astype(bf16)) for x, (xh, _), p in zip(guesses, splits, prods)
        ]
    return guesses


def inverse_kernel(pts, node_pts, o1, o2, o3, o4, a_high, a_low, b_high, b_low, spread_tile):
    features = pts.shape[0]
    half = o1.shape[1]
    node = node_pts[...]
    left, right = lifted(node)
    spread_tile[...] = kernel_of(left, lifted(pts[...])[1], features).astype(bf16)
    grams = [kernel_of(left, right, features)]
    own = node[:, :half]
    for other in (o1, o2, o3, o4):
        left, right = lifted(jnp.concatenate([own, other[...]], axis=1))
        grams.append(kernel_of(left, right, features))
    found = invert(grams)
    a_high[...], a_low[...] = split(found[0])
    for k in range(4):
        b_high[k], b_low[k] = split(SHIFT * found[k + 1][:, :half])


def inverses(points, node_pts, others):
    n = points.shape[1]
    s = node_pts.shape[1]
    return pl.pallas_call(
        inverse_kernel,
        out_shape=(
            jax.ShapeDtypeStruct((s, s), bf16),
            jax.ShapeDtypeStruct((s, s), bf16),
            jax.ShapeDtypeStruct((4, s, s // 2), bf16),
            jax.ShapeDtypeStruct((4, s, s // 2), bf16),
            jax.ShapeDtypeStruct((s, n), bf16),
        ),
        in_specs=[VMEM] * 6,
        out_specs=(VMEM,) * 5,
        compiler_params=params(),
        name="inverses",
    )(points, node_pts, *others)


def pair_of(lists, counts, i):
    slots = lists.shape[1]
    clusters = lists.shape[0]
    g = i // slots
    listed = lists[g, i % slots]
    way = listed // clusters - lists[0, 0] // clusters
    cols = pl.multiple_of((listed % clusters) * CLUSTER_PTS, CLUSTER_PTS)
    own_cols = pl.multiple_of(g * CLUSTER_PTS, CLUSTER_PTS)
    return (i % slots) < counts[g], way, pl.ds(cols, CLUSTER_PTS), pl.ds(own_cols, CLUSTER_PTS)


def own_kernel(lists, counts, pts, w, targets, out, left, right, tile):
    features = pts.shape[0]
    left[...], right[...] = lifted(pts[...])
    out[...] = targets[...].astype(f32) - RIDGE * w[...].astype(f32)

    def step(i, carry):
        live, way, cols, own = pair_of(lists, counts, i)

        @pl.when(live & (way == 0))
        def _():
            tile[...] = kernel_of(left[:, cols], right[:, own], features).astype(bf16)
            out[:, own] -= mm(w[:, cols], tile[...])

        return carry

    lax.fori_loop(0, lists.shape[0] * lists.shape[1], step, 0)


def own_near(points, weights, targets, near_lists, tile_counts):
    features, n = points.shape
    return pl.pallas_call(
        own_kernel,
        out_shape=jax.ShapeDtypeStruct(weights.shape, f32),
        in_specs=[SMEM, SMEM, VMEM, VMEM, VMEM],
        out_specs=VMEM,
        scratch_shapes=[
            pltpu.VMEM((features + 16, n), bf16),
            pltpu.VMEM((features + 16, n), bf16),
            pltpu.VMEM((CLUSTER_PTS, CLUSTER_PTS), bf16),
        ],
        compiler_params=params(),
        name="own_near",
    )(near_lists, tile_counts, points, weights, targets)


def tiles_kernel(lists, counts, pts, before, after, out, lb, la, right):
    features = pts.shape[0]
    right[...] = lifted(pts[...])[1]
    lb[...] = lifted(before[...])[0]
    la[...] = lifted(after[...])[0]

    def step(i, carry):
        live, way, cols, own = pair_of(lists, counts, i)

        @pl.when(live & (way < 0))
        def _():
            out[i] = kernel_of(lb[:, cols], right[:, own], features).astype(bf16)

        @pl.when(live & (way > 0))
        def _():
            out[i] = kernel_of(la[:, cols], right[:, own], features).astype(bf16)

        return carry

    lax.fori_loop(0, lists.shape[0] * lists.shape[1], step, 0)


def near_tiles(points, before, after, near_lists, tile_counts):
    features, n = points.shape
    pairs = near_lists.shape[0] * near_lists.shape[1]
    head = pl.BlockSpec((features, n), lambda i: (0, 0))
    return pl.pallas_call(
        tiles_kernel,
        out_shape=jax.ShapeDtypeStruct((pairs, CLUSTER_PTS, CLUSTER_PTS), bf16),
        grid=(1,),
        in_specs=[SMEM, SMEM, VMEM, head, head],
        out_specs=VMEM,
        scratch_shapes=[pltpu.VMEM((features + 16, n), bf16)] * 3,
        compiler_params=params(),
        name="near_tiles",
    )(near_lists, tile_counts, points, before, after)


def near_kernel(skip, lists, counts, base, before, after, tiles, pick, a_high, a_low, res, sol, kept):
    rows = base.shape[0]
    half = kept.shape[1]
    res[...] = base[...]

    def step(i, carry):
        live, way, cols, own = pair_of(lists, counts, i)

        @pl.when(live & (way < 0))
        def _():
            res[:, own] -= mm(before[skip : skip + rows, cols], tiles[i])

        @pl.when(live & (way > 0))
        def _():
            res[:, own] -= mm(after[skip : skip + rows, cols], tiles[i])

        return carry

    lax.fori_loop(0, lists.shape[0] * lists.shape[1], step, 0)
    high, low = split(res[...])
    node_high = mm(high, pick[...]).astype(bf16)
    node_low = mm(low, pick[...]).astype(bf16)
    solved = mm(node_high, a_high[...]) + (mm(node_high, a_low[...]) + mm(node_low, a_high[...]))
    sol[...] = solved
    kept[...] = solved[:, :half]


def near_part(base, first, rows, skip, before, after, tiles, pick, a_high, a_low, near_lists, tile_counts):
    n = base.shape[1]
    s = pick.shape[1]
    return pl.pallas_call(
        functools.partial(near_kernel, skip),
        out_shape=(
            jax.ShapeDtypeStruct((rows, n), f32),
            jax.ShapeDtypeStruct((rows, s), f32),
            jax.ShapeDtypeStruct((rows, s // 2), f32),
        ),
        grid=(1,),
        in_specs=[
            SMEM,
            SMEM,
            pl.BlockSpec((rows, n), lambda i: (first // rows, 0)),
            VMEM,
            VMEM,
            VMEM,
            VMEM,
            VMEM,
            VMEM,
        ],
        out_specs=(VMEM, VMEM, VMEM),
        compiler_params=params(32),
        name="near_part",
    )(near_lists, tile_counts, base, before, after, tiles, pick, a_high, a_low)


def level_kernel(level, own, other, b_high, b_low, out):
    half = own.shape[1]
    total = None
    for at, piece in ((0, own), (half, other)):
        high, low = split(piece[...])
        bh = b_high[level, at : at + half, :]
        bl = b_low[level, at : at + half, :]
        term = mm(high, bh) + (mm(high, bl) + mm(low, bh))
        total = term if total is None else total + term
    out[...] = total


def level_step(level, own, other, b_high, b_low):
    return pl.pallas_call(
        functools.partial(level_kernel, level),
        out_shape=jax.ShapeDtypeStruct(own.shape, f32),
        in_specs=[VMEM] * 4,
        out_specs=VMEM,
        compiler_params=params(),
        name="level_step",
    )(own, other, b_high, b_low)


def partner(value, stride):
    size = lax.axis_size("leaf")
    pairs = [(i, i ^ stride) for i in range(0, size, stride)]
    return lax.ppermute(value, "leaf", pairs)


def climb(kept, b_high, b_low):
    found = []
    value = kept
    for level in range(4):
        other = partner(value, 1 << level)
        value = level_step(level, value, other, b_high, b_low)
        found.append(value)
    return found


def out_kernel(lists, res, sol, c1, c2, c3, c4, tile, pick, *refs):
    out = refs[-1]
    half = c1.shape[1]
    clusters = lists.shape[0]
    leaf = (lists[0, 0] // clusters) % 16
    inject = c1[...]
    for level, part in ((1, c2), (2, c3), (3, c4)):
        inject = inject + jnp.where(leaf % (1 << level) == 0, part[...], 0.0)
    solved = sol[...]
    corr = jnp.concatenate([solved[:, :half] + inject, solved[:, half:]], axis=1)
    high, low = split(corr)
    spread = mm(high, tile[...])
    spread = spread + mm_t(high, pick[...]) + mm_t(low, pick[...])
    out[...] = res[...] * (1.0 / (1.0 + RIDGE)) + spread


def finish(whole, first, res, sol, parts, tile, pick, near_lists, total_rows):
    rows, n = res.shape
    extra = [] if whole is None else [whole]
    return pl.pallas_call(
        out_kernel,
        out_shape=jax.ShapeDtypeStruct((total_rows, n), f32),
        grid=(1,),
        in_specs=[SMEM] + [VMEM] * 8 + [pl.BlockSpec(memory_space=pl.ANY)] * len(extra),
        out_specs=pl.BlockSpec((rows, n), lambda i: (first // rows, 0)),
        input_output_aliases={9: 0} if extra else {},
        compiler_params=params(32),
        name="finish",
    )(near_lists, res, sol, *parts, tile, pick, *extra)


def shifted(value, by):
    size = lax.axis_size("clus")
    pairs = [(i, i + by) for i in range(size) if 0 <= i + by < size]
    return lax.ppermute(value, "clus", pairs)


def on_device(points, weights, targets, near_lists, tile_counts, skeleton):
    features = points.shape[0]
    rows = weights.shape[0]
    early = rows - LATE_ROWS
    first = jnp.concatenate([points, weights[:early]], axis=0)
    second = weights[early:]
    before_1, after_1 = shifted(first, 1), shifted(first, -1)
    before_2, after_2 = shifted(second, 1), shifted(second, -1)

    pick, node_pts, kept_pts = prep(points, skeleton)
    others = []
    size = lax.axis_size("leaf")
    for level in range(4):
        stride = 1 << level
        others.append(lax.ppermute(kept_pts, "leaf", [(i, i ^ stride) for i in range(size)]))
    base = own_near(points, weights, targets, near_lists, tile_counts)
    a_high, a_low, b_high, b_low, tile = inverses(points, node_pts, others)
    tiles = near_tiles(points, before_1, after_1, near_lists, tile_counts)

    whole = None
    for at, count, skip, before, after in (
        (0, early, features, before_1, after_1),
        (early, LATE_ROWS, 0, before_2, after_2),
    ):
        res, sol, kept = near_part(
            base, at, count, skip, before, after, tiles, pick, a_high, a_low, near_lists, tile_counts
        )
        parts = climb(kept, b_high, b_low)
        whole = finish(whole, at, res, sol, parts, tile, pick, near_lists, rows)
    return whole


def solution(mesh):
    split_cols = P(None, ("clus", "leaf"))
    split_rows = P(("clus", "leaf"), None)
    placed = (split_cols, split_cols, split_cols, split_rows, P(("clus", "leaf")), split_rows)
    return jax.shard_map(
        on_device, mesh=mesh, in_specs=placed, out_specs=split_cols, check_vma=False
    )
```

```python
import functools

import jax
import jax.numpy as jnp
from jax import lax
from jax.experimental import pallas as pl
from jax.experimental.pallas import tpu as pltpu
from jax.sharding import PartitionSpec as P


CLUSTER_PTS = 512
N_LEAF = 16
RIDGE = 0.5
SHIFT = 4.0
EARLY_ROWS = 192
COARSE_STEPS = 4
FINE_STEPS = 2

f32 = jnp.float32
bf16 = jnp.bfloat16
MIB = 1 << 20
VMEM = pl.BlockSpec(memory_space=pltpu.VMEM)
SMEM = pl.BlockSpec(memory_space=pltpu.SMEM)


def mm(a, b):
    return jnp.dot(a, b, preferred_element_type=f32)


def split(a):
    high = a.astype(bf16)
    return high, (a - high.astype(f32)).astype(bf16)


def lifted(x):
    wide = x.astype(f32)
    half = -0.5 * jnp.sum(wide * wide, axis=0, keepdims=True)
    high = half.astype(bf16).astype(f32)
    rest = half - high
    mid = rest.astype(bf16).astype(f32)
    low = rest - mid
    row = lax.broadcasted_iota(jnp.int32, (16, x.shape[1]), 0)

    def tail(at, ones):
        out = jnp.where((row >= ones) & (row < ones + 3), 1.0, 0.0)
        out = jnp.where(row == at, high, out)
        out = jnp.where(row == at + 1, mid, out)
        return jnp.where(row == at + 2, low, out).astype(bf16)

    left = jnp.concatenate([x, tail(0, 3)], axis=0)
    right = jnp.concatenate([x, tail(3, 0)], axis=0)
    return left, right


def kernel_of(left, right, features):
    half = lax.dot_general(left, right, (((0,), (0,)), ((), ())), preferred_element_type=f32)
    return jnp.exp((4.0 / features) * half)


def leaf_of(lists):
    return (lists[0, 0] // lists.shape[0]) % N_LEAF


def params(mib=24):
    return pltpu.CompilerParams(vmem_limit_bytes=mib * MIB)


def prep_kernel(*refs):
    srcs, (pick, note, kept), dsts, sems = refs[:4], refs[4:7], refs[7:11], refs[11]
    copies = [pltpu.make_async_copy(a, b, sems.at[k]) for k, (a, b) in enumerate(zip(srcs, dsts))]
    for copy in copies:
        copy.start()
    for copy in copies:
        copy.wait()
    lists, counts, pts, skel = dsts
    features, n = pts.shape
    s = skel.shape[1]
    clusters, slots = lists.shape
    chosen = skel[...]
    row = lax.broadcasted_iota(jnp.int32, (n, s), 0)
    picked = jnp.where(row == chosen, 1.0, 0.0).astype(bf16)
    pick[...] = picked
    gathered = mm(pts[...], picked).astype(bf16)
    note[:features, :] = gathered
    kept[...] = gathered[:, : s // 2]
    home = chosen // CLUSTER_PTS
    line = lax.broadcasted_iota(jnp.int32, (16, s), 0)
    flags = jnp.zeros((16, s), f32)
    for g in range(clusters):
        for slot in range(slots):
            listed = lists[g, slot]
            way = listed // clusters - lists[0, 0] // clusters
            begin = jnp.where(way < 0, 0, jnp.where(way > 0, clusters, 2 * clusters))
            at = jnp.where(slot < counts[g], begin + listed % clusters, -1)
            flags = jnp.where((line == at) & (home == g), 1.0, flags)
    note[features:, :] = flags.astype(bf16)


def prep(near_lists, tile_counts, points, skeleton):
    features, n = points.shape
    s = skeleton.shape[1]
    return pl.pallas_call(
        prep_kernel,
        out_shape=(
            jax.ShapeDtypeStruct((n, s), bf16),
            jax.ShapeDtypeStruct((features + 16, s), bf16),
            jax.ShapeDtypeStruct((features, s // 2), bf16),
        ),
        in_specs=[pl.BlockSpec(memory_space=pltpu.HBM)] * 4,
        out_specs=(VMEM, VMEM, VMEM),
        scratch_shapes=[
            pltpu.SMEM(near_lists.shape, jnp.int32),
            pltpu.SMEM(tile_counts.shape, jnp.int32),
            pltpu.VMEM(points.shape, bf16),
            pltpu.VMEM(skeleton.shape, jnp.int32),
            pltpu.SemaphoreType.DMA((4,)),
        ],
        compiler_params=params(),
        name="prep",
    )(near_lists, tile_counts, points, skeleton)


def invert(grams, between=()):
    between = list(between)
    share = -(-len(between) // (COARSE_STEPS + FINE_STEPS))

    def work():
        for _ in range(share):
            if between:
                between.pop(0)()

    s = grams[0].shape[0]
    eye = jnp.where(
        lax.broadcasted_iota(jnp.int32, (s, s), 0) == lax.broadcasted_iota(jnp.int32, (s, s), 1),
        1.0,
        0.0,
    ).astype(f32)
    parts, guesses, gaps = [], [], []
    for gram in grams:
        gram = gram + SHIFT * eye
        top = jnp.max(jnp.sum(gram, axis=0, keepdims=True), axis=1, keepdims=True)
        alpha = 2.0 / (top + SHIFT)
        gap = (top - SHIFT) / (top + SHIFT)
        gain = 2.0 / (2.0 - gap * gap)
        parts.append(split(gram))
        guesses.append((gain * alpha) * (2.0 * eye - alpha * gram))
        gaps.append(0.5 * gain * gap * gap)
    for _ in range(COARSE_STEPS):
        lows = [x.astype(bf16) for x in guesses]
        prods = [mm(gh, x) + mm(gl, x) for (gh, gl), x in zip(parts, lows)]
        work()
        gains = [2.0 / (2.0 - gap * gap) for gap in gaps]
        guesses = [
            gain * mm(x, (2.0 * eye - p).astype(bf16)) for gain, x, p in zip(gains, lows, prods)
        ]
        gaps = [0.5 * gain * gap * gap for gain, gap in zip(gains, gaps)]
    for _ in range(FINE_STEPS):
        splits = [split(x) for x in guesses]
        prods = [
            mm(gh, xh) + (mm(gh, xl) + mm(gl, xh)) for (gh, gl), (xh, xl) in zip(parts, splits)
        ]
        work()
        guesses = [
            x + mm(xh, (eye - p).astype(bf16)) for x, (xh, _), p in zip(guesses, splits, prods)
        ]
    while between:
        between.pop(0)()
    return guesses


def tree_part(total, w, left, right, ref, begin, j):
    features = ref.shape[0] - 16
    cols = slice(j * CLUSTER_PTS, (j + 1) * CLUSTER_PTS)
    flags = ref[features + begin + j : features + begin + j + 1, :].astype(f32)
    tile = kernel_of(left[:, cols], right, features) * flags
    term = mm(w[:, cols], tile.astype(bf16))
    if j == 0:
        total[...] = term
    else:
        total[...] += term


def solve_rows(values, high, low):
    vh, vl = split(values)
    return mm(vh, high) + (mm(vh, low) + mm(vl, high))


def inverse_kernel(pts, w, targets, pick, note, kept, o1, o2, o3, o4, mine, a_high, a_low, b_high, b_low, left, total):
    features, half = kept.shape
    clusters = pts.shape[1] // CLUSTER_PTS
    left[...] = lifted(pts[...])[0]
    own = kept[...]
    node_left, node_right = lifted(note[:features, :])
    grams = [kernel_of(node_left, node_right, features)]
    for other in (o1, o2, o3, o4):
        pair_left, pair_right = lifted(jnp.concatenate([own, other[...]], axis=1))
        grams.append(kernel_of(pair_left, pair_right, features))
    jobs = [
        functools.partial(tree_part, total, w, left, node_right, note, 2 * clusters, j)
        for j in range(clusters)
    ]

    def rest():
        total[...] = mm(targets[...], pick[...]) - RIDGE * mm(w[...], pick[...]) - total[...]

    found = invert(grams, jobs + [rest])
    ah, al = split(found[0])
    a_high[...], a_low[...] = ah, al
    for k in range(4):
        b_high[k], b_low[k] = split(SHIFT * found[k + 1][:, :half])
    mine[...] = solve_rows(total[...], ah[:, :half], al[:, :half])


def inverses(points, weights, targets, pick, note, kept, others):
    features, n = points.shape
    rows = weights.shape[0]
    half = kept.shape[1]
    s = 2 * half
    part = jax.ShapeDtypeStruct((4, s, half), bf16)
    full = jax.ShapeDtypeStruct((s, s), bf16)
    return pl.pallas_call(
        inverse_kernel,
        out_shape=(jax.ShapeDtypeStruct((rows, half), f32), full, full, part, part),
        in_specs=[VMEM] * 10,
        out_specs=(VMEM,) * 5,
        scratch_shapes=[pltpu.VMEM((features + 16, n), bf16), pltpu.VMEM((rows, s), f32)],
        compiler_params=params(),
        name="inverses",
    )(points, weights, targets, pick, note, kept, *others)


def push_kernel(pts, w, note_b, note_a, to_b, to_a, left, total):
    features, n = pts.shape
    half = to_b.shape[1]
    clusters = n // CLUSTER_PTS
    left[...] = lifted(pts[...])[0]
    notes = ((note_b, clusters), (note_a, 0))
    grams, jobs = [], []
    for k, (ref, begin) in enumerate(notes):
        node_left, node_right = lifted(ref[:features, :])
        grams.append(kernel_of(node_left, node_right, features))
        jobs += [
            functools.partial(tree_part, total.at[k], w, left, node_right, ref, begin, j)
            for j in range(clusters)
        ]
    for k, found in enumerate(invert(grams, jobs)):
        high, low = split(found[:, :half])
        (to_b, to_a)[k][...] = solve_rows(total[k], high, low)


def push(points, weights, note_b, note_a):
    features, n = points.shape
    rows = weights.shape[0]
    s = note_b.shape[1]
    return pl.pallas_call(
        push_kernel,
        out_shape=(jax.ShapeDtypeStruct((rows, s // 2), f32),) * 2,
        in_specs=[VMEM] * 4,
        out_specs=(VMEM,) * 2,
        scratch_shapes=[pltpu.VMEM((features + 16, n), bf16), pltpu.VMEM((2, rows, s), f32)],
        compiler_params=params(),
        name="push",
    )(points, weights, note_b, note_a)


def join_kernel(mine, from_b, from_a, out):
    out[...] = mine[...] - from_b[...] - from_a[...]


def join(mine, from_b, from_a):
    return pl.pallas_call(
        join_kernel,
        out_shape=jax.ShapeDtypeStruct(mine.shape, f32),
        in_specs=[VMEM] * 3,
        out_specs=VMEM,
        compiler_params=params(),
        name="join",
    )(mine, from_b, from_a)


def pair_of(lists, counts, i):
    slots = lists.shape[1]
    clusters = lists.shape[0]
    g = i // slots
    listed = lists[g, i % slots]
    way = listed // clusters - lists[0, 0] // clusters
    cols = pl.multiple_of((listed % clusters) * CLUSTER_PTS, CLUSTER_PTS)
    own_cols = pl.multiple_of(g * CLUSTER_PTS, CLUSTER_PTS)
    return (i % slots) < counts[g], way, pl.ds(cols, CLUSTER_PTS), pl.ds(own_cols, CLUSTER_PTS)


def own_kernel(lists, counts, pts, note, w, targets, pick, out, spread_tile, place, left, right, tile):
    features = pts.shape[0]
    left[...], right[...] = lifted(pts[...])
    node_left = lifted(note[:features, :])[0]
    spread_tile[...] = kernel_of(node_left, right[...], features).astype(bf16)
    place[...] = pick[...].T
    out[...] = targets[...].astype(f32) - RIDGE * w[...].astype(f32)

    def step(i, carry):
        live, way, cols, own = pair_of(lists, counts, i)

        @pl.when(live & (way == 0))
        def _():
            tile[...] = kernel_of(left[:, cols], right[:, own], features).astype(bf16)
            out[:, own] -= mm(w[:, cols], tile[...])

        return carry

    lax.fori_loop(0, lists.shape[0] * lists.shape[1], step, 0)


def own_near(points, note, weights, targets, pick, near_lists, tile_counts):
    features, n = points.shape
    return pl.pallas_call(
        own_kernel,
        out_shape=(
            jax.ShapeDtypeStruct(weights.shape, f32),
            jax.ShapeDtypeStruct((note.shape[1], n), bf16),
            jax.ShapeDtypeStruct((note.shape[1], n), bf16),
        ),
        in_specs=[SMEM, SMEM] + [VMEM] * 5,
        out_specs=(VMEM, VMEM, VMEM),
        scratch_shapes=[
            pltpu.VMEM((features + 16, n), bf16),
            pltpu.VMEM((features + 16, n), bf16),
            pltpu.VMEM((CLUSTER_PTS, CLUSTER_PTS), bf16),
        ],
        compiler_params=params(),
        name="own_near",
    )(near_lists, tile_counts, points, note, weights, targets, pick)


def tiles_kernel(lists, counts, pts, before, after, out, lb, la, right):
    features = pts.shape[0]
    right[...] = lifted(pts[...])[1]
    lb[...] = lifted(before[...])[0]
    la[...] = lifted(after[...])[0]

    def step(i, carry):
        live, way, cols, own = pair_of(lists, counts, i)

        @pl.when(live & (way < 0))
        def _():
            out[i] = kernel_of(lb[:, cols], right[:, own], features).astype(bf16)

        @pl.when(live & (way > 0))
        def _():
            out[i] = kernel_of(la[:, cols], right[:, own], features).astype(bf16)

        return carry

    lax.fori_loop(0, lists.shape[0] * lists.shape[1], step, 0)


def near_tiles(points, before, after, near_lists, tile_counts):
    features, n = points.shape
    pairs = near_lists.shape[0] * near_lists.shape[1]
    head = pl.BlockSpec((features, n), lambda i: (0, 0))
    return pl.pallas_call(
        tiles_kernel,
        out_shape=jax.ShapeDtypeStruct((pairs, CLUSTER_PTS, CLUSTER_PTS), bf16),
        grid=(1,),
        in_specs=[SMEM, SMEM, VMEM, head, head],
        out_specs=VMEM,
        scratch_shapes=[pltpu.VMEM((features + 16, n), bf16)] * 3,
        compiler_params=params(),
        name="near_tiles",
    )(near_lists, tile_counts, points, before, after)


def near_kernel(first, skip, lists, counts, base, before, after, tiles, pick, a_high, a_low, res, sol):
    rows = res.shape[0]
    res[...] = base[first : first + rows, :]

    def step(i, carry):
        live, way, cols, own = pair_of(lists, counts, i)

        @pl.when(live & (way < 0))
        def _():
            res[:, own] -= mm(before[skip : skip + rows, cols], tiles[i])

        @pl.when(live & (way > 0))
        def _():
            res[:, own] -= mm(after[skip : skip + rows, cols], tiles[i])

        return carry

    lax.fori_loop(0, lists.shape[0] * lists.shape[1], step, 0)
    high, low = split(res[...])
    node = mm(jnp.concatenate([high, low], axis=0), pick[...]).astype(bf16)
    both = mm(node, a_high[...])
    sol[...] = both[:rows] + (mm(node[:rows], a_low[...]) + both[rows:])


def near_part(first, rows, skip, base, before, after, tiles, pick, a_high, a_low, near_lists, tile_counts):
    n = base.shape[1]
    s = pick.shape[1]
    return pl.pallas_call(
        functools.partial(near_kernel, first, skip),
        out_shape=(jax.ShapeDtypeStruct((rows, n), f32), jax.ShapeDtypeStruct((rows, s), f32)),
        in_specs=[SMEM, SMEM] + [VMEM] * 7,
        out_specs=(VMEM, VMEM),
        compiler_params=params(),
        name="near_part",
    )(near_lists, tile_counts, base, before, after, tiles, pick, a_high, a_low)


def joint(own, other, b_high, b_low, at):
    half = own.shape[1]
    total = None
    for begin, piece in ((0, own), (half, other)):
        high, low = split(piece[...])
        bh = b_high[at, begin : begin + half, :]
        bl = b_low[at, begin : begin + half, :]
        term = mm(high, bh) + (mm(high, bl) + mm(low, bh))
        total = term if total is None else total + term
    return total


def level_kernel(at, own, other, b_high, b_low, out):
    out[...] = joint(own, other, b_high, b_low, at)


def level_step(at, own, other, b_high, b_low):
    return pl.pallas_call(
        functools.partial(level_kernel, at),
        out_shape=jax.ShapeDtypeStruct(own.shape, f32),
        in_specs=[VMEM] * 4,
        out_specs=VMEM,
        compiler_params=params(),
        name="level_step",
    )(own, other, b_high, b_low)


def among_leaves(value, pairs):
    return lax.ppermute(value, "leaf", pairs)


def out_kernel(cuts, lists, *refs):
    parts = refs[: 2 * len(cuts)]
    v1, v2, v3, w4, b_high, b_low, tile, place, out, buf, sems = refs[2 * len(cuts) :]
    half = v1.shape[1]
    leaf = leaf_of(lists)
    inject = v1[...]
    inject = inject + jnp.where(leaf % 2 == 0, v2[...], 0.0)
    inject = inject + jnp.where(leaf % 4 == 0, v3[...], 0.0)
    inject = inject + jnp.where(leaf % 8 == 0, joint(v3, w4, b_high, b_low, 3), 0.0)
    copies = []
    at = 0
    for k, blocks in enumerate(cuts):
        res, sol = parts[2 * k : 2 * k + 2]
        inner = 0
        for rows in blocks:
            solved = sol[inner : inner + rows, :]
            corr = jnp.concatenate([solved[:, :half] + inject[at : at + rows], solved[:, half:]], axis=1)
            high, low = split(corr)
            spread = mm(high, tile[...])
            spread = spread + mm(high, place[...]) + mm(low, place[...])
            buf[at : at + rows, :] = res[inner : inner + rows, :] * (1.0 / (1.0 + RIDGE)) + spread
            copy = pltpu.make_async_copy(
                buf.at[pl.ds(at, rows)], out.at[pl.ds(at, rows)], sems.at[len(copies)]
            )
            copy.start()
            copies.append(copy)
            at += rows
            inner += rows
    for copy in copies:
        copy.wait()


def finish(cuts, near_lists, parts, rest):
    total = sum(sum(blocks) for blocks in cuts)
    count = sum(len(blocks) for blocks in cuts)
    n = parts[0].shape[1]
    return pl.pallas_call(
        functools.partial(out_kernel, cuts),
        out_shape=jax.ShapeDtypeStruct((total, n), f32),
        in_specs=[SMEM] + [VMEM] * (len(parts) + len(rest)),
        out_specs=pl.BlockSpec(memory_space=pl.ANY),
        scratch_shapes=[pltpu.VMEM((total, n), f32), pltpu.SemaphoreType.DMA((count,))],
        compiler_params=params(),
        name="finish",
    )(near_lists, *parts, *rest)


def shifted(value, by):
    size = lax.axis_size("clus")
    pairs = [(i, i + by) for i in range(size) if 0 <= i + by < size]
    return lax.ppermute(value, "clus", pairs)


def both_ways(value):
    return shifted(value, 1), shifted(value, -1)


def on_device(points, weights, targets, near_lists, tile_counts, skeleton):
    features = points.shape[0]
    rows = weights.shape[0]
    late = rows - EARLY_ROWS
    size = lax.axis_size("leaf")
    steps = [[(i, i ^ (1 << k)) for i in range(0, size, 1 << k)] for k in range(4)]

    pick, note, kept = prep(near_lists, tile_counts, points, skeleton)
    note_b, note_a = both_ways(note)
    first = jnp.concatenate([points, weights[:EARLY_ROWS]], axis=0)
    before_1, after_1 = both_ways(first)
    to_b, to_a = push(points, weights, note_b, note_a)
    from_b = shifted(to_a, 1)
    from_a = shifted(to_b, -1)
    second = weights[EARLY_ROWS:]
    before_2, after_2 = both_ways(second)
    swaps = [[(i, i ^ (1 << k)) for i in range(size)] for k in range(4)]
    others = [among_leaves(kept, swaps[k]) for k in range(4)]
    mine, a_high, a_low, b_high, b_low = inverses(
        points, weights, targets, pick, note, kept, others
    )
    v0 = join(mine, from_b, from_a)

    base, tile, place = own_near(points, note, weights, targets, pick, near_lists, tile_counts)
    tiles = near_tiles(points, before_1, after_1, near_lists, tile_counts)
    shared = (tiles, pick, a_high, a_low, near_lists, tile_counts)
    res_1, sol_1 = near_part(0, EARLY_ROWS, features, base, before_1, after_1, *shared)
    res_2, sol_2 = near_part(EARLY_ROWS, late, 0, base, before_2, after_2, *shared)

    v1 = level_step(0, v0, among_leaves(v0, steps[0]), b_high, b_low)
    v2 = level_step(1, v1, among_leaves(v1, steps[1]), b_high, b_low)
    v3 = level_step(2, v2, among_leaves(v2, steps[2]), b_high, b_low)
    w4 = among_leaves(v3, steps[3])
    cuts = ((EARLY_ROWS,), (late // 2, late // 2))
    return finish(
        cuts, near_lists, (res_1, sol_1, res_2, sol_2), (v1, v2, v3, w4, b_high, b_low, tile, place)
    )


def solution(mesh):
    split_cols = P(None, ("clus", "leaf"))
    split_rows = P(("clus", "leaf"), None)
    placed = (split_cols, split_cols, split_cols, split_rows, P(("clus", "leaf")), split_rows)

    return jax.shard_map(
        on_device, mesh=mesh, in_specs=placed, out_specs=split_cols, check_vma=False
    )
```

```python
import functools

import jax
import jax.numpy as jnp
from jax import lax
from jax.experimental import pallas as pl
from jax.experimental.pallas import tpu as pltpu
from jax.sharding import PartitionSpec as P


CLUSTER_PTS = 512
N_LEAF = 16
RIDGE = 0.5
SHIFT = 4.0
EARLY_ROWS = 224
COARSE_STEPS = 4
FINE_STEPS = 2

f32 = jnp.float32
bf16 = jnp.bfloat16
MIB = 1 << 20
VMEM = pl.BlockSpec(memory_space=pltpu.VMEM)
SMEM = pl.BlockSpec(memory_space=pltpu.SMEM)


def mm(a, b):
    return jnp.dot(a, b, preferred_element_type=f32)


def split(a):
    high = a.astype(bf16)
    return high, (a - high.astype(f32)).astype(bf16)


def lifted(x):
    wide = x.astype(f32)
    half = -0.5 * jnp.sum(wide * wide, axis=0, keepdims=True)
    high = half.astype(bf16).astype(f32)
    rest = half - high
    mid = rest.astype(bf16).astype(f32)
    low = rest - mid
    row = lax.broadcasted_iota(jnp.int32, (16, x.shape[1]), 0)

    def tail(at, ones):
        out = jnp.where((row >= ones) & (row < ones + 3), 1.0, 0.0)
        out = jnp.where(row == at, high, out)
        out = jnp.where(row == at + 1, mid, out)
        return jnp.where(row == at + 2, low, out).astype(bf16)

    left = jnp.concatenate([x, tail(0, 3)], axis=0)
    right = jnp.concatenate([x, tail(3, 0)], axis=0)
    return left, right


def kernel_of(left, right, features):
    half = lax.dot_general(left, right, (((0,), (0,)), ((), ())), preferred_element_type=f32)
    return jnp.exp((4.0 / features) * half)


def leaf_of(lists):
    return (lists[0, 0] // lists.shape[0]) % N_LEAF


def params(mib=24):
    return pltpu.CompilerParams(vmem_limit_bytes=mib * MIB)


def prep_kernel(*refs):
    srcs, (pick, note, kept), dsts, sems = refs[:3], refs[3:6], refs[6:9], refs[9]
    copies = [pltpu.make_async_copy(a, b, sems.at[k]) for k, (a, b) in enumerate(zip(srcs, dsts))]
    for copy in copies:
        copy.start()
    for copy in copies:
        copy.wait()
    lists, pts, skel = dsts
    features, n = pts.shape
    s = skel.shape[1]
    clusters, slots = lists.shape
    chosen = skel[...]
    row = lax.broadcasted_iota(jnp.int32, (n, s), 0)
    picked = jnp.where(row == chosen, 1.0, 0.0).astype(bf16)
    pick[...] = picked
    gathered = mm(pts[...], picked).astype(bf16)
    note[:features, :] = gathered
    kept[...] = gathered[:, : s // 2]
    home = chosen // CLUSTER_PTS
    line = lax.broadcasted_iota(jnp.int32, (16, s), 0)
    flags = jnp.zeros((16, s), f32)
    for g in range(clusters):
        for slot in range(slots):
            listed = lists[g, slot]
            way = listed // clusters - lists[0, 0] // clusters
            begin = jnp.where(way < 0, 0, jnp.where(way > 0, clusters, 2 * clusters))
            at = jnp.where(is_live(lists, g, slot), begin + listed % clusters, -1)
            flags = jnp.where((line == at) & (home == g), 1.0, flags)
    note[features:, :] = flags.astype(bf16)


def prep(near_lists, points, skeleton):
    features, n = points.shape
    s = skeleton.shape[1]
    return pl.pallas_call(
        prep_kernel,
        out_shape=(
            jax.ShapeDtypeStruct((n, s), bf16),
            jax.ShapeDtypeStruct((features + 16, s), bf16),
            jax.ShapeDtypeStruct((features, s // 2), bf16),
        ),
        in_specs=[pl.BlockSpec(memory_space=pltpu.HBM)] * 3,
        out_specs=(VMEM, VMEM, VMEM),
        scratch_shapes=[
            pltpu.SMEM(near_lists.shape, jnp.int32),
            pltpu.VMEM(points.shape, bf16),
            pltpu.VMEM(skeleton.shape, jnp.int32),
            pltpu.SemaphoreType.DMA((3,)),
        ],
        compiler_params=params(60),
        name="prep",
    )(near_lists, points, skeleton)


def invert(grams, between=(), whole=0):
    between = list(between)
    share = -(-len(between) // (COARSE_STEPS + FINE_STEPS))

    def work():
        for _ in range(share):
            if between:
                between.pop(0)()

    s = grams[0].shape[0]
    eye = jnp.where(
        lax.broadcasted_iota(jnp.int32, (s, s), 0) == lax.broadcasted_iota(jnp.int32, (s, s), 1),
        1.0,
        0.0,
    ).astype(f32)
    parts, guesses, gaps = [], [], []
    for gram in grams:
        gram = gram + SHIFT * eye
        top = jnp.max(jnp.sum(gram, axis=0, keepdims=True), axis=1, keepdims=True)
        alpha = 2.0 / (top + SHIFT)
        gap = (top - SHIFT) / (top + SHIFT)
        gain = 2.0 / (2.0 - gap * gap)
        parts.append(split(gram))
        guesses.append((gain * alpha) * (2.0 * eye - alpha * gram))
        gaps.append(0.5 * gain * gap * gap)
    for _ in range(COARSE_STEPS):
        lows = [x.astype(bf16) for x in guesses]
        prods = [mm(gh, x) for (gh, _), x in zip(parts, lows)]
        work()
        gains = [2.0 / (2.0 - gap * gap) for gap in gaps]
        guesses = [
            gain * mm(x, (2.0 * eye - p).astype(bf16)) for gain, x, p in zip(gains, lows, prods)
        ]
        gaps = [0.5 * gain * gap * gap for gain, gap in zip(gains, gaps)]
    for step in range(FINE_STEPS):
        splits = [split(x) for x in guesses]
        wide = [s if step < FINE_STEPS - 1 or k < whole else s // 2 for k in range(len(grams))]
        prods = [
            mm(gh, xh[:, :c]) + (mm(gh, xl[:, :c]) + mm(gl, xh[:, :c]))
            for (gh, gl), (xh, xl), c in zip(parts, splits, wide)
        ]
        work()
        guesses = [
            x[:, :c] + mm(xh, (eye[:, :c] - p).astype(bf16))
            for x, (xh, _), p, c in zip(guesses, splits, prods, wide)
        ]
    while between:
        between.pop(0)()
    return guesses


def tree_part(total, w, left, right, ref, begin, j):
    features = ref.shape[0] - 16
    cols = slice(j * CLUSTER_PTS, (j + 1) * CLUSTER_PTS)
    flags = ref[features + begin + j : features + begin + j + 1, :].astype(f32)
    tile = kernel_of(left[:, cols], right, features) * flags
    term = mm(w[:, cols], tile.astype(bf16))
    if j == 0:
        total[...] = term
    else:
        total[...] += term


def solve_rows(values, high, low):
    vh, vl = split(values)
    return mm(vh, high) + (mm(vh, low) + mm(vl, high))


def inverse_kernel(pts, w, targets, pick, note, kept, o1, o2, o3, o4, from_b, from_a, start, a_high, a_low, b_high, b_low, left, total):
    features, half = kept.shape
    clusters = pts.shape[1] // CLUSTER_PTS
    left[...] = lifted(pts[...])[0]
    own = kept[...]
    node_left, node_right = lifted(note[:features, :])
    grams = [kernel_of(node_left, node_right, features)]
    for other in (o1, o2, o3, o4):
        pair_left, pair_right = lifted(jnp.concatenate([own, other[...]], axis=1))
        grams.append(kernel_of(pair_left, pair_right, features))
    jobs = [
        functools.partial(tree_part, total, w, left, node_right, note, 2 * clusters, j)
        for j in range(clusters)
    ]

    def rest():
        total[...] = mm(targets[...], pick[...]) - RIDGE * mm(w[...], pick[...]) - total[...]

    found = invert(grams, jobs + [rest], 1)
    ah, al = split(found[0])
    a_high[...], a_low[...] = ah, al
    for k in range(4):
        b_high[k], b_low[k] = split(SHIFT * found[k + 1])
    start[...] = solve_rows(total[...], ah[:, :half], al[:, :half]) - from_b[...] - from_a[...]


def inverses(points, weights, targets, pick, note, kept, others, from_b, from_a):
    features, n = points.shape
    rows = weights.shape[0]
    half = kept.shape[1]
    s = 2 * half
    part = jax.ShapeDtypeStruct((4, s, half), bf16)
    full = jax.ShapeDtypeStruct((s, s), bf16)
    return pl.pallas_call(
        inverse_kernel,
        out_shape=(jax.ShapeDtypeStruct((rows, half), f32), full, full, part, part),
        in_specs=[VMEM] * 12,
        out_specs=(VMEM,) * 5,
        scratch_shapes=[pltpu.VMEM((features + 16, n), bf16), pltpu.VMEM((rows, s), f32)],
        compiler_params=params(),
        name="inverses",
    )(points, weights, targets, pick, note, kept, *others, from_b, from_a)


def push_kernel(pts, w, note_b, note_a, to_b, to_a, left, total):
    features, n = pts.shape
    clusters = n // CLUSTER_PTS
    left[...] = lifted(pts[...])[0]
    notes = ((note_b, clusters), (note_a, 0))
    grams, jobs = [], []
    for k, (ref, begin) in enumerate(notes):
        node_left, node_right = lifted(ref[:features, :])
        grams.append(kernel_of(node_left, node_right, features))
        jobs += [
            functools.partial(tree_part, total.at[k], w, left, node_right, ref, begin, j)
            for j in range(clusters)
        ]
    for k, found in enumerate(invert(grams, jobs)):
        high, low = split(found)
        (to_b, to_a)[k][...] = solve_rows(total[k], high, low)


def push(points, weights, note_b, note_a):
    features, n = points.shape
    rows = weights.shape[0]
    s = note_b.shape[1]
    return pl.pallas_call(
        push_kernel,
        out_shape=(jax.ShapeDtypeStruct((rows, s // 2), f32),) * 2,
        in_specs=[VMEM] * 4,
        out_specs=(VMEM,) * 2,
        scratch_shapes=[pltpu.VMEM((features + 16, n), bf16), pltpu.VMEM((2, rows, s), f32)],
        compiler_params=params(),
        name="push",
    )(points, weights, note_b, note_a)


def is_live(lists, g, slot):
    return (slot == 0) | (lists[g, slot] != lists[g, 0])


def pair_of(lists, i):
    slots = lists.shape[1]
    clusters = lists.shape[0]
    g = i // slots
    listed = lists[g, i % slots]
    way = listed // clusters - lists[0, 0] // clusters
    cols = pl.multiple_of((listed % clusters) * CLUSTER_PTS, CLUSTER_PTS)
    own_cols = pl.multiple_of(g * CLUSTER_PTS, CLUSTER_PTS)
    return is_live(lists, g, i % slots), way, pl.ds(cols, CLUSTER_PTS), pl.ds(own_cols, CLUSTER_PTS)


def own_kernel(lists, pts, w, targets, out, left, right, tile):
    features = pts.shape[0]
    left[...], right[...] = lifted(pts[...])
    out[...] = targets[...].astype(f32) - RIDGE * w[...].astype(f32)

    def step(i, carry):
        live, way, cols, own = pair_of(lists, i)

        @pl.when(live & (way == 0))
        def _():
            tile[...] = kernel_of(left[:, cols], right[:, own], features).astype(bf16)
            out[:, own] -= mm(w[:, cols], tile[...])

        return carry

    lax.fori_loop(0, lists.shape[0] * lists.shape[1], step, 0)


def own_near(points, weights, targets, near_lists):
    features, n = points.shape
    return pl.pallas_call(
        own_kernel,
        out_shape=jax.ShapeDtypeStruct(weights.shape, f32),
        in_specs=[SMEM] + [VMEM] * 3,
        out_specs=VMEM,
        scratch_shapes=[
            pltpu.VMEM((features + 16, n), bf16),
            pltpu.VMEM((features + 16, n), bf16),
            pltpu.VMEM((CLUSTER_PTS, CLUSTER_PTS), bf16),
        ],
        compiler_params=params(),
        name="own_near",
    )(near_lists, points, weights, targets)


def tables_kernel(pts, note, pick, spread_tile, place):
    features = pts.shape[0]
    node_left = lifted(note[:features, :])[0]
    spread_tile[...] = kernel_of(node_left, lifted(pts[...])[1], features).astype(bf16)
    place[...] = pick[...].T


def tables(points, note, pick):
    shape = jax.ShapeDtypeStruct((note.shape[1], points.shape[1]), bf16)
    return pl.pallas_call(
        tables_kernel,
        out_shape=(shape, shape),
        in_specs=[VMEM] * 3,
        out_specs=(VMEM, VMEM),
        compiler_params=params(),
        name="tables",
    )(points, note, pick)


def tiles_kernel(lists, pts, before, after, out, lb, la, right):
    features = pts.shape[0]
    right[...] = lifted(pts[...])[1]
    lb[...] = lifted(before[...])[0]
    la[...] = lifted(after[...])[0]

    def step(i, carry):
        live, way, cols, own = pair_of(lists, i)

        @pl.when(live & (way < 0))
        def _():
            out[i] = kernel_of(lb[:, cols], right[:, own], features).astype(bf16)

        @pl.when(live & (way > 0))
        def _():
            out[i] = kernel_of(la[:, cols], right[:, own], features).astype(bf16)

        return carry

    lax.fori_loop(0, lists.shape[0] * lists.shape[1], step, 0)


def near_tiles(points, before, after, near_lists):
    features, n = points.shape
    pairs = near_lists.shape[0] * near_lists.shape[1]
    head = pl.BlockSpec((features, n), lambda i: (0, 0))
    return pl.pallas_call(
        tiles_kernel,
        out_shape=jax.ShapeDtypeStruct((pairs, CLUSTER_PTS, CLUSTER_PTS), bf16),
        grid=(1,),
        in_specs=[SMEM, VMEM, head, head],
        out_specs=VMEM,
        scratch_shapes=[pltpu.VMEM((features + 16, n), bf16)] * 3,
        compiler_params=params(),
        name="near_tiles",
    )(near_lists, points, before, after)


def near_kernel(first, skip, lists, base, before, after, tiles, pick, a_high, a_low, res, sol):
    rows = res.shape[0]
    res[...] = base[first : first + rows, :]

    def step(i, carry):
        live, way, cols, own = pair_of(lists, i)

        @pl.when(live & (way < 0))
        def _():
            res[:, own] -= mm(before[skip : skip + rows, cols], tiles[i])

        @pl.when(live & (way > 0))
        def _():
            res[:, own] -= mm(after[skip : skip + rows, cols], tiles[i])

        return carry

    lax.fori_loop(0, lists.shape[0] * lists.shape[1], step, 0)
    high, low = split(res[...])
    node = mm(jnp.concatenate([high, low], axis=0), pick[...]).astype(bf16)
    both = mm(node, a_high[...])
    sol[...] = both[:rows] + (mm(node[:rows], a_low[...]) + both[rows:])


def near_part(first, rows, skip, base, before, after, tiles, pick, a_high, a_low, near_lists):
    n = base.shape[1]
    s = pick.shape[1]
    return pl.pallas_call(
        functools.partial(near_kernel, first, skip),
        out_shape=(jax.ShapeDtypeStruct((rows, n), f32), jax.ShapeDtypeStruct((rows, s), f32)),
        in_specs=[SMEM] + [VMEM] * 7,
        out_specs=(VMEM, VMEM),
        compiler_params=params(),
        name="near_part",
    )(near_lists, base, before, after, tiles, pick, a_high, a_low)


def joint(own, other, b_high, b_low, at):
    half = own.shape[1]
    total = None
    for begin, piece in ((0, own), (half, other)):
        bh = b_high[at, begin : begin + half, :]
        bl = b_low[at, begin : begin + half, :]
        if piece.dtype == bf16:
            term = mm(piece[...], bh) + mm(piece[...], bl)
        else:
            high, low = split(piece[...])
            term = mm(high, bh) + (mm(high, bl) + mm(low, bh))
        total = term if total is None else total + term
    return total


def level_kernel(at, own, other, b_high, b_low, out):
    out[...] = joint(own, other, b_high, b_low, at)


def level_step(at, own, other, b_high, b_low):
    return pl.pallas_call(
        functools.partial(level_kernel, at),
        out_shape=jax.ShapeDtypeStruct(own.shape, f32),
        in_specs=[VMEM] * 4,
        out_specs=VMEM,
        compiler_params=params(),
        name="level_step",
    )(own, other, b_high, b_low)


def among_leaves(value, pairs):
    return lax.ppermute(value, "leaf", pairs)


def settle_kernel(cuts, lists, *refs):
    parts = refs[: 2 * len(cuts)]
    v1, v2, v3, place, ready, corr = refs[2 * len(cuts) :]
    half = v1.shape[1]
    leaf = leaf_of(lists)
    at = 0
    for k, rows in enumerate(cuts):
        res, sol = parts[2 * k : 2 * k + 2]
        here = slice(at, at + rows)
        inject = v1[here, :] + jnp.where(leaf % 2 == 0, v2[here, :], 0.0)
        inject = inject + jnp.where(leaf % 4 == 0, v3[here, :], 0.0)
        corr[here, :half] = sol[:, :half] + inject
        corr[here, half:] = sol[:, half:]
        high, low = split(corr[here, :])
        ready[here, :] = res[...] * (1.0 / (1.0 + RIDGE)) + mm(high, place[...]) + mm(low, place[...])
        at += rows


def settle(cuts, near_lists, parts, rest):
    total = sum(cuts)
    n = parts[0].shape[1]
    return pl.pallas_call(
        functools.partial(settle_kernel, cuts),
        out_shape=(
            jax.ShapeDtypeStruct((total, n), f32),
            jax.ShapeDtypeStruct((total, parts[1].shape[1]), f32),
        ),
        in_specs=[SMEM] + [VMEM] * (len(parts) + len(rest)),
        out_specs=(VMEM, VMEM),
        compiler_params=params(),
        name="settle",
    )(near_lists, *parts, *rest)


def out_kernel(blocks, lists, ready, corr, v3, w4, b_high, b_low, tile, place, out, buf, sems):
    half = v3.shape[1]
    leaf = leaf_of(lists)
    last = jnp.where(leaf % 8 == 0, joint(v3, w4, b_high, b_low, 3), 0.0)
    last_high, last_low = split(last)
    twice = jnp.concatenate([place[:half, :], place[:half, :]], axis=0)
    copies = []
    at = 0
    for k, rows in enumerate(blocks):
        here = slice(at, at + rows)
        full = jnp.concatenate([corr[here, :half] + last[here], corr[here, half:]], axis=1)
        added = jnp.concatenate([last_high[here], last_low[here]], axis=1)
        buf[here, :] = ready[here, :] + mm(full.astype(bf16), tile[...]) + mm(added, twice)
        copy = pltpu.make_async_copy(buf.at[pl.ds(at, rows)], out.at[pl.ds(at, rows)], sems.at[k])
        copy.start()
        copies.append(copy)
        at += rows
    for copy in copies:
        copy.wait()


def finish(blocks, near_lists, *args):
    total, n = args[0].shape
    return pl.pallas_call(
        functools.partial(out_kernel, blocks),
        out_shape=jax.ShapeDtypeStruct((total, n), f32),
        in_specs=[SMEM] + [VMEM] * len(args),
        out_specs=pl.BlockSpec(memory_space=pl.ANY),
        scratch_shapes=[pltpu.VMEM((total, n), f32), pltpu.SemaphoreType.DMA((len(blocks),))],
        compiler_params=params(),
        name="finish",
    )(near_lists, *args)


def shifted(value, by):
    size = lax.axis_size("clus")
    pairs = [(i, i + by) for i in range(size) if 0 <= i + by < size]
    return lax.ppermute(value, "clus", pairs)


def both_ways(value):
    return shifted(value, 1), shifted(value, -1)


def on_device(points, weights, targets, near_lists, tile_counts, skeleton):
    features = points.shape[0]
    rows = weights.shape[0]
    late = rows - EARLY_ROWS
    size = lax.axis_size("leaf")
    steps = [[(i, i ^ (1 << k)) for i in range(0, size, 1 << k)] for k in range(4)]

    pick, note, kept = prep(near_lists, points, skeleton)
    note_b, note_a = both_ways(note)
    first = jnp.concatenate([points, weights[:EARLY_ROWS]], axis=0)
    before_1, after_1 = both_ways(first)
    to_b, to_a = push(points, weights, note_b, note_a)
    from_b = shifted(to_a, 1)
    from_a = shifted(to_b, -1)
    second = weights[EARLY_ROWS:]
    before_2, after_2 = both_ways(second)
    swaps = [[(i, i ^ (1 << k)) for i in range(size)] for k in range(4)]
    others = [among_leaves(kept, swaps[k]) for k in range(4)]
    v0, a_high, a_low, b_high, b_low = inverses(
        points, weights, targets, pick, note, kept, others, from_b, from_a
    )

    base = own_near(points, weights, targets, near_lists)
    tiles = near_tiles(points, before_1, after_1, near_lists)
    shared = (tiles, pick, a_high, a_low, near_lists)
    res_1, sol_1 = near_part(0, EARLY_ROWS, features, base, before_1, after_1, *shared)
    res_2, sol_2 = near_part(EARLY_ROWS, late, 0, base, before_2, after_2, *shared)

    tile, place = tables(points, note, pick)

    v1 = level_step(0, v0, among_leaves(v0, steps[0]), b_high, b_low)
    v2 = level_step(1, v1, among_leaves(v1.astype(bf16), steps[1]), b_high, b_low)
    v3 = level_step(2, v2, among_leaves(v2.astype(bf16), steps[2]), b_high, b_low)
    w4 = among_leaves(v3.astype(bf16), steps[3])
    ready, corr = settle(
        (EARLY_ROWS, late), near_lists, (res_1, sol_1, res_2, sol_2), (v1, v2, v3, place)
    )
    return finish((192, 192, 128), near_lists, ready, corr, v3, w4, b_high, b_low, tile, place)


def solution(mesh):
    split_cols = P(None, ("clus", "leaf"))
    split_rows = P(("clus", "leaf"), None)
    placed = (split_cols, split_cols, split_cols, split_rows, P(("clus", "leaf")), split_rows)

    return jax.shard_map(
        on_device, mesh=mesh, in_specs=placed, out_specs=split_cols, check_vma=False
    )
```

```python
import functools

import jax
import jax.numpy as jnp
from jax import lax
from jax.experimental import pallas as pl
from jax.experimental.pallas import tpu as pltpu
from jax.sharding import PartitionSpec as P


CLUSTER_PTS = 512
N_LEAF = 16
RIDGE = 0.5
SHIFT = 4.0
EARLY_ROWS = 192
COARSE_STEPS = 4
FINE_STEPS = 2

f32 = jnp.float32
bf16 = jnp.bfloat16
MIB = 1 << 20
VMEM = pl.BlockSpec(memory_space=pltpu.VMEM)
SMEM = pl.BlockSpec(memory_space=pltpu.SMEM)


def mm(a, b):
    return jnp.dot(a, b, preferred_element_type=f32)


def split(a):
    high = a.astype(bf16)
    return high, (a - high.astype(f32)).astype(bf16)


def lifted(x):
    wide = x.astype(f32)
    half = -0.5 * jnp.sum(wide * wide, axis=0, keepdims=True)
    high = half.astype(bf16).astype(f32)
    rest = half - high
    mid = rest.astype(bf16).astype(f32)
    low = rest - mid
    row = lax.broadcasted_iota(jnp.int32, (16, x.shape[1]), 0)

    def tail(at, ones):
        out = jnp.where((row >= ones) & (row < ones + 3), 1.0, 0.0)
        out = jnp.where(row == at, high, out)
        out = jnp.where(row == at + 1, mid, out)
        return jnp.where(row == at + 2, low, out).astype(bf16)

    left = jnp.concatenate([x, tail(0, 3)], axis=0).T
    right = jnp.concatenate([x, tail(3, 0)], axis=0)
    return left, right


def kernel_of(left, right, features):
    return jnp.exp((4.0 / features) * mm(left, right))


def leaf_of(lists):
    return (lists[0, 0] // lists.shape[0]) % N_LEAF


def params(mib=24):
    return pltpu.CompilerParams(vmem_limit_bytes=mib * MIB)


def prep_kernel(*refs):
    srcs, (pick, note, kept), dsts, sems = refs[:3], refs[3:6], refs[6:9], refs[9]
    copies = [pltpu.make_async_copy(a, b, sems.at[k]) for k, (a, b) in enumerate(zip(srcs, dsts))]
    for copy in copies:
        copy.start()
    for copy in copies:
        copy.wait()
    lists, pts, skel = dsts
    features, n = pts.shape
    s = skel.shape[1]
    clusters, slots = lists.shape
    chosen = skel[...]
    row = lax.broadcasted_iota(jnp.int32, (n, s), 0)
    picked = jnp.where(row == chosen, 1.0, 0.0).astype(bf16)
    pick[...] = picked
    gathered = mm(pts[...], picked).astype(bf16)
    note[:features, :] = gathered
    kept[...] = gathered[:, : s // 2]
    home = chosen // CLUSTER_PTS
    line = lax.broadcasted_iota(jnp.int32, (16, s), 0)
    flags = jnp.zeros((16, s), f32)
    for g in range(clusters):
        for slot in range(slots):
            listed = lists[g, slot]
            way = listed // clusters - lists[0, 0] // clusters
            begin = jnp.where(way < 0, 0, jnp.where(way > 0, clusters, 2 * clusters))
            at = jnp.where(is_live(lists, g, slot), begin + listed % clusters, -1)
            flags = jnp.where((line == at) & (home == g), 1.0, flags)
    note[features:, :] = flags.astype(bf16)


def prep(near_lists, points, skeleton):
    features, n = points.shape
    s = skeleton.shape[1]
    return pl.pallas_call(
        prep_kernel,
        out_shape=(
            jax.ShapeDtypeStruct((n, s), bf16),
            jax.ShapeDtypeStruct((features + 16, s), bf16),
            jax.ShapeDtypeStruct((features, s // 2), bf16),
        ),
        in_specs=[pl.BlockSpec(memory_space=pltpu.HBM)] * 3,
        out_specs=(VMEM, VMEM, VMEM),
        scratch_shapes=[
            pltpu.SMEM(near_lists.shape, jnp.int32),
            pltpu.VMEM(points.shape, bf16),
            pltpu.VMEM(skeleton.shape, jnp.int32),
            pltpu.SemaphoreType.DMA((3,)),
        ],
        compiler_params=params(),
        name="prep",
    )(near_lists, points, skeleton)


def invert(grams, between=(), whole=0):
    between = list(between)
    share = -(-len(between) // (COARSE_STEPS + FINE_STEPS))

    def work():
        for _ in range(share):
            if between:
                between.pop(0)()

    s = grams[0].shape[0]
    eye = jnp.where(
        lax.broadcasted_iota(jnp.int32, (s, s), 0) == lax.broadcasted_iota(jnp.int32, (s, s), 1),
        1.0,
        0.0,
    ).astype(f32)
    parts, guesses, gaps = [], [], []
    for gram in grams:
        gram = gram + SHIFT * eye
        top = jnp.max(jnp.sum(gram, axis=0, keepdims=True), axis=1, keepdims=True)
        alpha = 2.0 / (top + SHIFT)
        gap = (top - SHIFT) / (top + SHIFT)
        gain = 2.0 / (2.0 - gap * gap)
        parts.append(split(gram))
        guesses.append((gain * alpha) * (2.0 * eye - alpha * gram))
        gaps.append(0.5 * gain * gap * gap)
    for _ in range(COARSE_STEPS):
        lows = [x.astype(bf16) for x in guesses]
        prods = [mm(gh, x) for (gh, _), x in zip(parts, lows)]
        work()
        gains = [2.0 / (2.0 - gap * gap) for gap in gaps]
        guesses = [
            gain * mm(x, (2.0 * eye - p).astype(bf16)) for gain, x, p in zip(gains, lows, prods)
        ]
        gaps = [0.5 * gain * gap * gap for gain, gap in zip(gains, gaps)]
    for step in range(FINE_STEPS):
        splits = [split(x) for x in guesses]
        wide = [s if step < FINE_STEPS - 1 or k < whole else s // 2 for k in range(len(grams))]
        prods = [
            mm(gh, xh[:, :c]) + (mm(gh, xl[:, :c]) + mm(gl, xh[:, :c]))
            for (gh, gl), (xh, xl), c in zip(parts, splits, wide)
        ]
        work()
        guesses = [
            x[:, :c] + mm(xh, (eye[:, :c] - p).astype(bf16))
            for x, (xh, _), p, c in zip(guesses, splits, prods, wide)
        ]
    while between:
        between.pop(0)()
    return guesses


def tree_part(total, w, left, right, ref, begin, j):
    features = ref.shape[0] - 16
    cols = slice(j * CLUSTER_PTS, (j + 1) * CLUSTER_PTS)
    flags = ref[features + begin + j : features + begin + j + 1, :].astype(f32)
    tile = kernel_of(left[cols, :], right, features) * flags
    term = mm(w[:, cols], tile.astype(bf16))
    if j == 0:
        total[...] = term
    else:
        total[...] += term


def solve_rows(values, high, low):
    vh, vl = split(values)
    return mm(vh, high) + (mm(vh, low) + mm(vl, high))


def inverse_kernel(pts, w, targets, pick, note, kept, o1, o2, o3, o4, mine, a_high, a_low, b_high, b_low, left, total):
    features, half = kept.shape
    clusters = pts.shape[1] // CLUSTER_PTS
    left[...] = lifted(pts[...])[0]
    own = kept[...]
    node_left, node_right = lifted(note[:features, :])
    grams = [kernel_of(node_left, node_right, features)]
    for other in (o1, o2, o3, o4):
        pair_left, pair_right = lifted(jnp.concatenate([own, other[...]], axis=1))
        grams.append(kernel_of(pair_left, pair_right, features))
    jobs = [
        functools.partial(tree_part, total, w, left, node_right, note, 2 * clusters, j)
        for j in range(clusters)
    ]

    def rest():
        total[...] = mm(targets[...], pick[...]) - RIDGE * mm(w[...], pick[...]) - total[...]

    found = invert(grams, jobs + [rest], 1)
    ah, al = split(found[0])
    a_high[...], a_low[...] = ah, al
    for k in range(4):
        b_high[k], b_low[k] = split(SHIFT * found[k + 1])
    mine[...] = solve_rows(total[...], ah[:, :half], al[:, :half])


def inverses(points, weights, targets, pick, note, kept, others):
    features, n = points.shape
    rows = weights.shape[0]
    half = kept.shape[1]
    s = 2 * half
    part = jax.ShapeDtypeStruct((4, s, half), bf16)
    full = jax.ShapeDtypeStruct((s, s), bf16)
    return pl.pallas_call(
        inverse_kernel,
        out_shape=(jax.ShapeDtypeStruct((rows, half), f32), full, full, part, part),
        in_specs=[VMEM] * 10,
        out_specs=(VMEM,) * 5,
        scratch_shapes=[pltpu.VMEM((n, features + 16), bf16), pltpu.VMEM((rows, s), f32)],
        compiler_params=params(),
        name="inverses",
    )(points, weights, targets, pick, note, kept, *others)


def push_kernel(pts, w, note_b, note_a, to_b, to_a, left, total):
    features, n = pts.shape
    clusters = n // CLUSTER_PTS
    left[...] = lifted(pts[...])[0]
    notes = ((note_b, clusters), (note_a, 0))
    grams, jobs = [], []
    for k, (ref, begin) in enumerate(notes):
        node_left, node_right = lifted(ref[:features, :])
        grams.append(kernel_of(node_left, node_right, features))
        jobs += [
            functools.partial(tree_part, total.at[k], w, left, node_right, ref, begin, j)
            for j in range(clusters)
        ]
    for k, found in enumerate(invert(grams, jobs)):
        high, low = split(found)
        (to_b, to_a)[k][...] = solve_rows(total[k], high, low)


def push(points, weights, note_b, note_a):
    features, n = points.shape
    rows = weights.shape[0]
    s = note_b.shape[1]
    return pl.pallas_call(
        push_kernel,
        out_shape=(jax.ShapeDtypeStruct((rows, s // 2), f32),) * 2,
        in_specs=[VMEM] * 4,
        out_specs=(VMEM,) * 2,
        scratch_shapes=[pltpu.VMEM((n, features + 16), bf16), pltpu.VMEM((2, rows, s), f32)],
        compiler_params=params(),
        name="push",
    )(points, weights, note_b, note_a)


def join_kernel(mine, from_b, from_a, out):
    out[...] = mine[...] - from_b[...] - from_a[...]


def join(mine, from_b, from_a):
    return pl.pallas_call(
        join_kernel,
        out_shape=jax.ShapeDtypeStruct(mine.shape, f32),
        in_specs=[VMEM] * 3,
        out_specs=VMEM,
        compiler_params=params(),
        name="join",
    )(mine, from_b, from_a)


def is_live(lists, g, slot):
    return (slot == 0) | (lists[g, slot] != lists[g, 0])


def pair_of(lists, i):
    slots = lists.shape[1]
    clusters = lists.shape[0]
    g = i // slots
    listed = lists[g, i % slots]
    way = listed // clusters - lists[0, 0] // clusters
    cols = pl.multiple_of((listed % clusters) * CLUSTER_PTS, CLUSTER_PTS)
    own_cols = pl.multiple_of(g * CLUSTER_PTS, CLUSTER_PTS)
    return is_live(lists, g, i % slots), way, pl.ds(cols, CLUSTER_PTS), pl.ds(own_cols, CLUSTER_PTS)


def own_kernel(lists, pts, w, targets, out, left, right, tile):
    features = pts.shape[0]
    left[...], right[...] = lifted(pts[...])
    slots = lists.shape[1]

    def step(i, carry):
        live, way, cols, own = pair_of(lists, i)

        @pl.when(live & (way == 0))
        def _():
            tile[...] = kernel_of(left[cols, :], right[:, own], features).astype(bf16)
            term = mm(w[:, cols], tile[...])

            @pl.when(i % slots == 0)
            def _():
                plain = targets[:, own].astype(f32) - RIDGE * w[:, own].astype(f32)
                out[:, own] = plain - term

            @pl.when(i % slots != 0)
            def _():
                out[:, own] -= term

        return carry

    lax.fori_loop(0, lists.shape[0] * slots, step, 0)


def own_near(points, weights, targets, near_lists):
    features, n = points.shape
    return pl.pallas_call(
        own_kernel,
        out_shape=jax.ShapeDtypeStruct(weights.shape, f32),
        in_specs=[SMEM] + [VMEM] * 3,
        out_specs=VMEM,
        scratch_shapes=[
            pltpu.VMEM((n, features + 16), bf16),
            pltpu.VMEM((features + 16, n), bf16),
            pltpu.VMEM((CLUSTER_PTS, CLUSTER_PTS), bf16),
        ],
        compiler_params=params(),
        name="own_near",
    )(near_lists, points, weights, targets)


def tables_kernel(pts, note, pick, spread_tile, place):
    features = pts.shape[0]
    node_left = lifted(note[:features, :])[0]
    spread_tile[...] = kernel_of(node_left, lifted(pts[...])[1], features).astype(bf16)
    place[...] = pick[...].T


def tables(points, note, pick):
    shape = jax.ShapeDtypeStruct((note.shape[1], points.shape[1]), bf16)
    return pl.pallas_call(
        tables_kernel,
        out_shape=(shape, shape),
        in_specs=[VMEM] * 3,
        out_specs=(VMEM, VMEM),
        compiler_params=params(),
        name="tables",
    )(points, note, pick)


def tiles_kernel(lists, pts, before, after, out, lb, la, right):
    features = pts.shape[0]
    right[...] = lifted(pts[...])[1]
    lb[...] = lifted(before[...])[0]
    la[...] = lifted(after[...])[0]

    def step(i, carry):
        live, way, cols, own = pair_of(lists, i)

        @pl.when(live & (way < 0))
        def _():
            out[i] = kernel_of(lb[cols, :], right[:, own], features).astype(bf16)

        @pl.when(live & (way > 0))
        def _():
            out[i] = kernel_of(la[cols, :], right[:, own], features).astype(bf16)

        return carry

    lax.fori_loop(0, lists.shape[0] * lists.shape[1], step, 0)


def near_tiles(points, before, after, near_lists):
    features, n = points.shape
    pairs = near_lists.shape[0] * near_lists.shape[1]
    head = pl.BlockSpec((features, n), lambda i: (0, 0))
    return pl.pallas_call(
        tiles_kernel,
        out_shape=jax.ShapeDtypeStruct((pairs, CLUSTER_PTS, CLUSTER_PTS), bf16),
        grid=(1,),
        in_specs=[SMEM, VMEM, head, head],
        out_specs=VMEM,
        scratch_shapes=[pltpu.VMEM((n, features + 16), bf16)] * 2
        + [pltpu.VMEM((features + 16, n), bf16)],
        compiler_params=params(),
        name="near_tiles",
    )(near_lists, points, before, after)


def near_kernel(first, skip, lists, base, before, after, tiles, pick, a_high, a_low, res, sol):
    rows = res.shape[0]
    res[...] = base[first : first + rows, :]

    def step(i, carry):
        live, way, cols, own = pair_of(lists, i)

        @pl.when(live & (way < 0))
        def _():
            res[:, own] -= mm(before[skip : skip + rows, cols], tiles[i])

        @pl.when(live & (way > 0))
        def _():
            res[:, own] -= mm(after[skip : skip + rows, cols], tiles[i])

        return carry

    lax.fori_loop(0, lists.shape[0] * lists.shape[1], step, 0)
    high, low = split(res[...])
    node = mm(jnp.concatenate([high, low], axis=0), pick[...]).astype(bf16)
    both = mm(node, a_high[...])
    sol[...] = both[:rows] + (mm(node[:rows], a_low[...]) + both[rows:])


def near_part(first, rows, skip, base, before, after, tiles, pick, a_high, a_low, near_lists):
    n = base.shape[1]
    s = pick.shape[1]
    return pl.pallas_call(
        functools.partial(near_kernel, first, skip),
        out_shape=(jax.ShapeDtypeStruct((rows, n), f32), jax.ShapeDtypeStruct((rows, s), f32)),
        in_specs=[SMEM] + [VMEM] * 7,
        out_specs=(VMEM, VMEM),
        compiler_params=params(),
        name="near_part",
    )(near_lists, base, before, after, tiles, pick, a_high, a_low)


def joint(own, other, b_high, b_low, at):
    half = own.shape[1]
    total = None
    for begin, piece in ((0, own), (half, other)):
        bh = b_high[at, begin : begin + half, :]
        bl = b_low[at, begin : begin + half, :]
        if piece.dtype == bf16:
            term = mm(piece[...], bh) + mm(piece[...], bl)
        else:
            high, low = split(piece[...])
            term = mm(high, bh) + (mm(high, bl) + mm(low, bh))
        total = term if total is None else total + term
    return total


def level_kernel(at, own, other, b_high, b_low, out):
    out[...] = joint(own, other, b_high, b_low, at)


def level_step(at, own, other, b_high, b_low):
    return pl.pallas_call(
        functools.partial(level_kernel, at),
        out_shape=jax.ShapeDtypeStruct(own.shape, f32),
        in_specs=[VMEM] * 4,
        out_specs=VMEM,
        compiler_params=params(),
        name="level_step",
    )(own, other, b_high, b_low)


def among_leaves(value, pairs):
    return lax.ppermute(value, "leaf", pairs)


def settle_kernel(cuts, lists, *refs):
    parts = refs[: 2 * len(cuts)]
    v1, v2, v3, place, ready, corr = refs[2 * len(cuts) :]
    half = v1.shape[1]
    leaf = leaf_of(lists)
    at = 0
    for k, rows in enumerate(cuts):
        res, sol = parts[2 * k : 2 * k + 2]
        here = slice(at, at + rows)
        inject = v1[here, :] + jnp.where(leaf % 2 == 0, v2[here, :], 0.0)
        inject = inject + jnp.where(leaf % 4 == 0, v3[here, :], 0.0)
        corr[here, :half] = sol[:, :half] + inject
        corr[here, half:] = sol[:, half:]
        high, low = split(corr[here, :])
        ready[here, :] = res[...] * (1.0 / (1.0 + RIDGE)) + mm(high, place[...]) + mm(low, place[...])
        at += rows


def settle(cuts, near_lists, parts, rest):
    total = sum(cuts)
    n = parts[0].shape[1]
    return pl.pallas_call(
        functools.partial(settle_kernel, cuts),
        out_shape=(
            jax.ShapeDtypeStruct((total, n), f32),
            jax.ShapeDtypeStruct((total, parts[1].shape[1]), f32),
        ),
        in_specs=[SMEM] + [VMEM] * (len(parts) + len(rest)),
        out_specs=(VMEM, VMEM),
        compiler_params=params(),
        name="settle",
    )(near_lists, *parts, *rest)


def out_kernel(blocks, lists, ready, corr, v3, w4, b_high, b_low, tile, place, out, buf, sems):
    half = v3.shape[1]
    leaf = leaf_of(lists)
    last = jnp.where(leaf % 8 == 0, joint(v3, w4, b_high, b_low, 3), 0.0)
    last_high, last_low = split(last)
    twice = jnp.concatenate([place[:half, :], place[:half, :]], axis=0)
    copies = []
    at = 0
    for k, rows in enumerate(blocks):
        here = slice(at, at + rows)
        full = jnp.concatenate([corr[here, :half] + last[here], corr[here, half:]], axis=1)
        added = jnp.concatenate([last_high[here], last_low[here]], axis=1)
        buf[here, :] = ready[here, :] + mm(full.astype(bf16), tile[...]) + mm(added, twice)
        copy = pltpu.make_async_copy(buf.at[pl.ds(at, rows)], out.at[pl.ds(at, rows)], sems.at[k])
        copy.start()
        copies.append(copy)
        at += rows
    for copy in copies:
        copy.wait()


def finish(blocks, near_lists, *args):
    total, n = args[0].shape
    return pl.pallas_call(
        functools.partial(out_kernel, blocks),
        out_shape=jax.ShapeDtypeStruct((total, n), f32),
        in_specs=[SMEM] + [VMEM] * len(args),
        out_specs=pl.BlockSpec(memory_space=pl.ANY),
        scratch_shapes=[pltpu.VMEM((total, n), f32), pltpu.SemaphoreType.DMA((len(blocks),))],
        compiler_params=params(),
        name="finish",
    )(near_lists, *args)


def shifted(value, by):
    size = lax.axis_size("clus")
    pairs = [(i, i + by) for i in range(size) if 0 <= i + by < size]
    return lax.ppermute(value, "clus", pairs)


def both_ways(value):
    return shifted(value, 1), shifted(value, -1)


def on_device(points, weights, targets, near_lists, tile_counts, skeleton):
    features = points.shape[0]
    rows = weights.shape[0]
    late = rows - EARLY_ROWS
    size = lax.axis_size("leaf")
    steps = [[(i, i ^ (1 << k)) for i in range(0, size, 1 << k)] for k in range(4)]

    pick, note, kept = prep(near_lists, points, skeleton)
    note_b, note_a = both_ways(note)
    first = jnp.concatenate([points, weights[:EARLY_ROWS]], axis=0)
    before_1, after_1 = both_ways(first)
    to_b, to_a = push(points, weights, note_b, note_a)
    from_b = shifted(to_a, 1)
    from_a = shifted(to_b, -1)
    second = weights[EARLY_ROWS:]
    before_2, after_2 = both_ways(second)
    swaps = [[(i, i ^ (1 << k)) for i in range(size)] for k in range(4)]
    others = [among_leaves(kept, swaps[k]) for k in range(4)]
    mine, a_high, a_low, b_high, b_low = inverses(
        points, weights, targets, pick, note, kept, others
    )

    v0 = join(mine, from_b, from_a)
    base = own_near(points, weights, targets, near_lists)
    tiles = near_tiles(points, before_1, after_1, near_lists)
    shared = (tiles, pick, a_high, a_low, near_lists)
    res_1, sol_1 = near_part(0, EARLY_ROWS, features, base, before_1, after_1, *shared)
    res_2, sol_2 = near_part(EARLY_ROWS, late, 0, base, before_2, after_2, *shared)

    tile, place = tables(points, note, pick)

    v1 = level_step(0, v0, among_leaves(v0, steps[0]), b_high, b_low)
    v2 = level_step(1, v1, among_leaves(v1.astype(bf16), steps[1]), b_high, b_low)
    v3 = level_step(2, v2, among_leaves(v2.astype(bf16), steps[2]), b_high, b_low)
    w4 = among_leaves(v3.astype(bf16), steps[3])
    ready, corr = settle(
        (EARLY_ROWS, late), near_lists, (res_1, sol_1, res_2, sol_2), (v1, v2, v3, place)
    )
    return finish((192, 192, 128), near_lists, ready, corr, v3, w4, b_high, b_low, tile, place)


def solution(mesh):
    split_cols = P(None, ("clus", "leaf"))
    split_rows = P(("clus", "leaf"), None)
    placed = (split_cols, split_cols, split_cols, split_rows, P(("clus", "leaf")), split_rows)

    return jax.shard_map(
        on_device, mesh=mesh, in_specs=placed, out_specs=split_cols, check_vma=False
    )
```

```python
import functools

import jax
import jax.numpy as jnp
from jax import lax
from jax.experimental import pallas as pl
from jax.experimental.pallas import tpu as pltpu
from jax.sharding import PartitionSpec as P


CLUSTER_PTS = 512
N_LEAF = 16
RIDGE = 0.5
SHIFT = 4.0
EARLY_ROWS = 192
COARSE_STEPS = 4
FINE_STEPS = 2

f32 = jnp.float32
bf16 = jnp.bfloat16
MIB = 1 << 20
VMEM = pl.BlockSpec(memory_space=pltpu.VMEM)
SMEM = pl.BlockSpec(memory_space=pltpu.SMEM)


def mm(a, b):
    return jnp.dot(a, b, preferred_element_type=f32)


def split(a):
    high = a.astype(bf16)
    return high, (a - high.astype(f32)).astype(bf16)


def lifted(x):
    wide = x.astype(f32)
    half = -0.5 * jnp.sum(wide * wide, axis=0, keepdims=True)
    high = half.astype(bf16).astype(f32)
    rest = half - high
    mid = rest.astype(bf16).astype(f32)
    low = rest - mid
    row = lax.broadcasted_iota(jnp.int32, (16, x.shape[1]), 0)

    def tail(at, ones):
        out = jnp.where((row >= ones) & (row < ones + 3), 1.0, 0.0)
        out = jnp.where(row == at, high, out)
        out = jnp.where(row == at + 1, mid, out)
        return jnp.where(row == at + 2, low, out).astype(bf16)

    left = jnp.concatenate([x, tail(0, 3)], axis=0).T
    right = jnp.concatenate([x, tail(3, 0)], axis=0)
    return left, right


def kernel_of(left, right, features):
    return jnp.exp((4.0 / features) * mm(left, right))


def leaf_of(lists):
    return (lists[0, 0] // lists.shape[0]) % N_LEAF


def params(mib=24):
    return pltpu.CompilerParams(vmem_limit_bytes=mib * MIB)


def prep_kernel(*refs):
    srcs, (pick, note, kept), dsts, sems = refs[:3], refs[3:6], refs[6:9], refs[9]
    copies = [pltpu.make_async_copy(a, b, sems.at[k]) for k, (a, b) in enumerate(zip(srcs, dsts))]
    for copy in copies:
        copy.start()
    for copy in copies:
        copy.wait()
    lists, pts, skel = dsts
    features, n = pts.shape
    s = skel.shape[1]
    clusters, slots = lists.shape
    chosen = skel[...]
    row = lax.broadcasted_iota(jnp.int32, (n, s), 0)
    picked = jnp.where(row == chosen, 1.0, 0.0).astype(bf16)
    pick[...] = picked
    gathered = mm(pts[...], picked).astype(bf16)
    note[:features, :] = gathered
    kept[...] = gathered[:, : s // 2]
    home = chosen // CLUSTER_PTS
    line = lax.broadcasted_iota(jnp.int32, (16, s), 0)
    flags = jnp.zeros((16, s), f32)
    for g in range(clusters):
        for slot in range(slots):
            listed = lists[g, slot]
            way = listed // clusters - lists[0, 0] // clusters
            begin = jnp.where(way < 0, 0, jnp.where(way > 0, clusters, 2 * clusters))
            at = jnp.where(is_live(lists, g, slot), begin + listed % clusters, -1)
            flags = jnp.where((line == at) & (home == g), 1.0, flags)
    note[features:, :] = flags.astype(bf16)


def prep(near_lists, points, skeleton):
    features, n = points.shape
    s = skeleton.shape[1]
    return pl.pallas_call(
        prep_kernel,
        out_shape=(
            jax.ShapeDtypeStruct((n, s), bf16),
            jax.ShapeDtypeStruct((features + 16, s), bf16),
            jax.ShapeDtypeStruct((features, s // 2), bf16),
        ),
        in_specs=[pl.BlockSpec(memory_space=pltpu.HBM)] * 3,
        out_specs=(VMEM, VMEM, VMEM),
        scratch_shapes=[
            pltpu.SMEM(near_lists.shape, jnp.int32),
            pltpu.VMEM(points.shape, bf16),
            pltpu.VMEM(skeleton.shape, jnp.int32),
            pltpu.SemaphoreType.DMA((3,)),
        ],
        compiler_params=params(),
        name="prep",
    )(near_lists, points, skeleton)


def invert(grams, between=(), whole=0):
    between = list(between)
    share = -(-len(between) // (COARSE_STEPS + FINE_STEPS))

    def work():
        for _ in range(share):
            if between:
                between.pop(0)()

    s = grams[0].shape[0]
    eye = jnp.where(
        lax.broadcasted_iota(jnp.int32, (s, s), 0) == lax.broadcasted_iota(jnp.int32, (s, s), 1),
        1.0,
        0.0,
    ).astype(f32)
    parts, guesses, gaps = [], [], []
    for gram in grams:
        gram = gram + SHIFT * eye
        top = jnp.max(jnp.sum(gram, axis=0, keepdims=True), axis=1, keepdims=True)
        alpha = 2.0 / (top + SHIFT)
        gap = (top - SHIFT) / (top + SHIFT)
        gain = 2.0 / (2.0 - gap * gap)
        parts.append(split(gram))
        guesses.append((gain * alpha) * (2.0 * eye - alpha * gram))
        gaps.append(0.5 * gain * gap * gap)
    for _ in range(COARSE_STEPS):
        lows = [x.astype(bf16) for x in guesses]
        prods = [mm(gh, x) for (gh, _), x in zip(parts, lows)]
        work()
        gains = [2.0 / (2.0 - gap * gap) for gap in gaps]
        guesses = [
            gain * mm(x, (2.0 * eye - p).astype(bf16)) for gain, x, p in zip(gains, lows, prods)
        ]
        gaps = [0.5 * gain * gap * gap for gain, gap in zip(gains, gaps)]
    for step in range(FINE_STEPS):
        splits = [split(x) for x in guesses]
        wide = [s if step < FINE_STEPS - 1 or k < whole else s // 2 for k in range(len(grams))]
        prods = [
            mm(gh, xh[:, :c]) + (mm(gh, xl[:, :c]) + mm(gl, xh[:, :c]))
            for (gh, gl), (xh, xl), c in zip(parts, splits, wide)
        ]
        work()
        guesses = [
            x[:, :c] + mm(xh, (eye[:, :c] - p).astype(bf16))
            for x, (xh, _), p, c in zip(guesses, splits, prods, wide)
        ]
    while between:
        between.pop(0)()
    return guesses


def tree_part(total, w, left, right, ref, begin, j, ridge=None):
    features = ref.shape[0] - 16
    cols = slice(j * CLUSTER_PTS, (j + 1) * CLUSTER_PTS)
    flags = ref[features + begin + j : features + begin + j + 1, :].astype(f32)
    tile = kernel_of(left[cols, :], right, features) * flags
    tile = tile.astype(bf16)
    if ridge is not None:
        tile = tile + RIDGE * ridge[cols, :]
    term = mm(w[:, cols], tile)
    if j == 0:
        total[...] = term
    else:
        total[...] += term


def solve_rows(values, high, low):
    vh, vl = split(values)
    return mm(vh, high) + (mm(vh, low) + mm(vl, high))


def inverse_kernel(pts, w, targets, pick, note, kept, o1, o2, o3, o4, mine, a_high, a_low, b_high, b_low, left, total):
    features, half = kept.shape
    clusters = pts.shape[1] // CLUSTER_PTS
    left[...] = lifted(pts[...])[0]
    own = kept[...]
    node_left, node_right = lifted(note[:features, :])
    grams = [kernel_of(node_left, node_right, features)]
    for other in (o1, o2, o3, o4):
        pair_left, pair_right = lifted(jnp.concatenate([own, other[...]], axis=1))
        grams.append(kernel_of(pair_left, pair_right, features))
    jobs = [
        functools.partial(tree_part, total, w, left, node_right, note, 2 * clusters, j, pick)
        for j in range(clusters)
    ]

    def rest():
        total[...] = mm(targets[...], pick[...]) - total[...]

    found = invert(grams, jobs + [rest], 1)
    ah, al = split(found[0])
    a_high[...], a_low[...] = ah, al
    for k in range(4):
        b_high[k], b_low[k] = split(SHIFT * found[k + 1])
    mine[...] = solve_rows(total[...], ah[:, :half], al[:, :half])


def inverses(points, weights, targets, pick, note, kept, others):
    features, n = points.shape
    rows = weights.shape[0]
    half = kept.shape[1]
    s = 2 * half
    part = jax.ShapeDtypeStruct((4, s, half), bf16)
    full = jax.ShapeDtypeStruct((s, s), bf16)
    return pl.pallas_call(
        inverse_kernel,
        out_shape=(jax.ShapeDtypeStruct((rows, half), f32), full, full, part, part),
        in_specs=[VMEM] * 10,
        out_specs=(VMEM,) * 5,
        scratch_shapes=[pltpu.VMEM((n, features + 16), bf16), pltpu.VMEM((rows, s), f32)],
        compiler_params=params(),
        name="inverses",
    )(points, weights, targets, pick, note, kept, *others)


def push_kernel(pts, w, note_b, note_a, to_b, to_a, left, total):
    features, n = pts.shape
    clusters = n // CLUSTER_PTS
    left[...] = lifted(pts[...])[0]
    notes = ((note_b, clusters), (note_a, 0))
    grams, jobs = [], []
    for k, (ref, begin) in enumerate(notes):
        node_left, node_right = lifted(ref[:features, :])
        grams.append(kernel_of(node_left, node_right, features))
        jobs += [
            functools.partial(tree_part, total.at[k], w, left, node_right, ref, begin, j)
            for j in range(clusters)
        ]
    for k, found in enumerate(invert(grams, jobs)):
        high, low = split(found)
        (to_b, to_a)[k][...] = solve_rows(total[k], high, low)


def push(points, weights, note_b, note_a):
    features, n = points.shape
    rows = weights.shape[0]
    s = note_b.shape[1]
    return pl.pallas_call(
        push_kernel,
        out_shape=(jax.ShapeDtypeStruct((rows, s // 2), f32),) * 2,
        in_specs=[VMEM] * 4,
        out_specs=(VMEM,) * 2,
        scratch_shapes=[pltpu.VMEM((n, features + 16), bf16), pltpu.VMEM((2, rows, s), f32)],
        compiler_params=params(),
        name="push",
    )(points, weights, note_b, note_a)


def join_kernel(mine, from_b, from_a, out):
    out[...] = mine[...] - from_b[...] - from_a[...]


def join(mine, from_b, from_a):
    return pl.pallas_call(
        join_kernel,
        out_shape=jax.ShapeDtypeStruct(mine.shape, f32),
        in_specs=[VMEM] * 3,
        out_specs=VMEM,
        compiler_params=params(),
        name="join",
    )(mine, from_b, from_a)


def is_live(lists, g, slot):
    return (slot == 0) | (lists[g, slot] != lists[g, 0])


def pair_of(lists, i):
    slots = lists.shape[1]
    clusters = lists.shape[0]
    g = i // slots
    listed = lists[g, i % slots]
    way = listed // clusters - lists[0, 0] // clusters
    cols = pl.multiple_of((listed % clusters) * CLUSTER_PTS, CLUSTER_PTS)
    own_cols = pl.multiple_of(g * CLUSTER_PTS, CLUSTER_PTS)
    return is_live(lists, g, i % slots), way, pl.ds(cols, CLUSTER_PTS), pl.ds(own_cols, CLUSTER_PTS)


def own_kernel(lists, pts, w, targets, out, left, right, tile):
    features = pts.shape[0]
    left[...], right[...] = lifted(pts[...])
    slots = lists.shape[1]

    def step(i, carry):
        live, way, cols, own = pair_of(lists, i)

        @pl.when(live & (way == 0))
        def _():
            tile[...] = kernel_of(left[cols, :], right[:, own], features).astype(bf16)
            term = mm(w[:, cols], tile[...])

            @pl.when(i % slots == 0)
            def _():
                plain = targets[:, own].astype(f32) - RIDGE * w[:, own].astype(f32)
                out[:, own] = plain - term

            @pl.when(i % slots != 0)
            def _():
                out[:, own] -= term

        return carry

    lax.fori_loop(0, lists.shape[0] * slots, step, 0)


def own_near(points, weights, targets, near_lists):
    features, n = points.shape
    return pl.pallas_call(
        own_kernel,
        out_shape=jax.ShapeDtypeStruct(weights.shape, f32),
        in_specs=[SMEM] + [VMEM] * 3,
        out_specs=VMEM,
        scratch_shapes=[
            pltpu.VMEM((n, features + 16), bf16),
            pltpu.VMEM((features + 16, n), bf16),
            pltpu.VMEM((CLUSTER_PTS, CLUSTER_PTS), bf16),
        ],
        compiler_params=params(),
        name="own_near",
    )(near_lists, points, weights, targets)


def tables_kernel(pts, note, pick, spread_tile, place):
    features = pts.shape[0]
    node_left = lifted(note[:features, :])[0]
    spread_tile[...] = kernel_of(node_left, lifted(pts[...])[1], features).astype(bf16)
    place[...] = pick[...].T


def tables(points, note, pick):
    shape = jax.ShapeDtypeStruct((note.shape[1], points.shape[1]), bf16)
    return pl.pallas_call(
        tables_kernel,
        out_shape=(shape, shape),
        in_specs=[VMEM] * 3,
        out_specs=(VMEM, VMEM),
        compiler_params=params(),
        name="tables",
    )(points, note, pick)


def tiles_kernel(lists, pts, before, after, out, lb, la, right):
    features = pts.shape[0]
    right[...] = lifted(pts[...])[1]
    lb[...] = lifted(before[...])[0]
    la[...] = lifted(after[...])[0]

    def step(i, carry):
        live, way, cols, own = pair_of(lists, i)

        @pl.when(live & (way < 0))
        def _():
            out[i] = kernel_of(lb[cols, :], right[:, own], features).astype(bf16)

        @pl.when(live & (way > 0))
        def _():
            out[i] = kernel_of(la[cols, :], right[:, own], features).astype(bf16)

        return carry

    lax.fori_loop(0, lists.shape[0] * lists.shape[1], step, 0)


def near_tiles(points, before, after, near_lists):
    features, n = points.shape
    pairs = near_lists.shape[0] * near_lists.shape[1]
    head = pl.BlockSpec((features, n), lambda i: (0, 0))
    return pl.pallas_call(
        tiles_kernel,
        out_shape=jax.ShapeDtypeStruct((pairs, CLUSTER_PTS, CLUSTER_PTS), bf16),
        grid=(1,),
        in_specs=[SMEM, VMEM, head, head],
        out_specs=VMEM,
        scratch_shapes=[pltpu.VMEM((n, features + 16), bf16)] * 2
        + [pltpu.VMEM((features + 16, n), bf16)],
        compiler_params=params(),
        name="near_tiles",
    )(near_lists, points, before, after)


def near_kernel(first, skip, lists, base, before, after, tiles, pick, a_high, a_low, res, sol):
    rows = res.shape[0]
    res[...] = base[first : first + rows, :]

    def step(i, carry):
        live, way, cols, own = pair_of(lists, i)

        @pl.when(live & (way < 0))
        def _():
            res[:, own] -= mm(before[skip : skip + rows, cols], tiles[i])

        @pl.when(live & (way > 0))
        def _():
            res[:, own] -= mm(after[skip : skip + rows, cols], tiles[i])

        return carry

    lax.fori_loop(0, lists.shape[0] * lists.shape[1], step, 0)
    high, low = split(res[...])
    node = mm(jnp.concatenate([high, low], axis=0), pick[...]).astype(bf16)
    both = mm(node, a_high[...])
    sol[...] = both[:rows] + (mm(node[:rows], a_low[...]) + both[rows:])


def near_part(first, rows, skip, base, before, after, tiles, pick, a_high, a_low, near_lists):
    n = base.shape[1]
    s = pick.shape[1]
    return pl.pallas_call(
        functools.partial(near_kernel, first, skip),
        out_shape=(jax.ShapeDtypeStruct((rows, n), f32), jax.ShapeDtypeStruct((rows, s), f32)),
        in_specs=[SMEM] + [VMEM] * 7,
        out_specs=(VMEM, VMEM),
        compiler_params=params(),
        name="near_part",
    )(near_lists, base, before, after, tiles, pick, a_high, a_low)


def joint(own, other, b_high, b_low, at):
    half = own.shape[1]
    total = None
    for begin, piece in ((0, own), (half, other)):
        bh = b_high[at, begin : begin + half, :]
        bl = b_low[at, begin : begin + half, :]
        if piece.dtype == bf16:
            term = mm(piece[...], bh) + mm(piece[...], bl)
        else:
            high, low = split(piece[...])
            term = mm(high, bh) + (mm(high, bl) + mm(low, bh))
        total = term if total is None else total + term
    return total


def level_kernel(at, own, other, b_high, b_low, out):
    out[...] = joint(own, other, b_high, b_low, at)


def level_step(at, own, other, b_high, b_low):
    return pl.pallas_call(
        functools.partial(level_kernel, at),
        out_shape=jax.ShapeDtypeStruct(own.shape, f32),
        in_specs=[VMEM] * 4,
        out_specs=VMEM,
        compiler_params=params(),
        name="level_step",
    )(own, other, b_high, b_low)


def among_leaves(value, pairs):
    return lax.ppermute(value, "leaf", pairs)


def settle_kernel(cuts, lists, *refs):
    parts = refs[: 2 * len(cuts)]
    v1, v2, v3, place, ready, corr = refs[2 * len(cuts) :]
    half = v1.shape[1]
    leaf = leaf_of(lists)
    at = 0
    for k, rows in enumerate(cuts):
        res, sol = parts[2 * k : 2 * k + 2]
        here = slice(at, at + rows)
        inject = v1[here, :] + jnp.where(leaf % 2 == 0, v2[here, :], 0.0)
        inject = inject + jnp.where(leaf % 4 == 0, v3[here, :], 0.0)
        corr[here, :half] = sol[:, :half] + inject
        corr[here, half:] = sol[:, half:]
        high, low = split(corr[here, :])
        ready[here, :] = res[...] * (1.0 / (1.0 + RIDGE)) + mm(high, place[...]) + mm(low, place[...])
        at += rows


def last_kernel(first, *refs):
    lists, base, before, after, tiles, pick, a_high, a_low = refs[:8]
    res_1, sol_1, v1, v2, v3, place, ready, corr, res, sol = refs[8:]
    near_kernel(first, 0, lists, base, before, after, tiles, pick, a_high, a_low, res, sol)
    cuts = (first, res.shape[0])
    settle_kernel(cuts, lists, res_1, sol_1, res, sol, v1, v2, v3, place, ready, corr)


def last_part(first, base, before, after, tiles, pick, a_high, a_low, near_lists, *rest):
    total, n = base.shape
    s = pick.shape[1]
    return pl.pallas_call(
        functools.partial(last_kernel, first),
        out_shape=(jax.ShapeDtypeStruct((total, n), f32), jax.ShapeDtypeStruct((total, s), f32)),
        in_specs=[SMEM] + [VMEM] * (7 + len(rest)),
        out_specs=(VMEM, VMEM),
        scratch_shapes=[pltpu.VMEM((total - first, n), f32), pltpu.VMEM((total - first, s), f32)],
        compiler_params=params(),
        name="last_part",
    )(near_lists, base, before, after, tiles, pick, a_high, a_low, *rest)


def out_kernel(blocks, lists, ready, corr, v3, w4, b_high, b_low, tile, place, out, buf, sems):
    half = v3.shape[1]
    leaf = leaf_of(lists)
    last = jnp.where(leaf % 8 == 0, joint(v3, w4, b_high, b_low, 3), 0.0)
    last_high, last_low = split(last)
    twice = jnp.concatenate([place[:half, :], place[:half, :]], axis=0)
    copies = []
    at = 0
    for k, rows in enumerate(blocks):
        here = slice(at, at + rows)
        full = jnp.concatenate([corr[here, :half] + last[here], corr[here, half:]], axis=1)
        added = jnp.concatenate([last_high[here], last_low[here]], axis=1)
        buf[here, :] = ready[here, :] + mm(full.astype(bf16), tile[...]) + mm(added, twice)
        copy = pltpu.make_async_copy(buf.at[pl.ds(at, rows)], out.at[pl.ds(at, rows)], sems.at[k])
        copy.start()
        copies.append(copy)
        at += rows
    for copy in copies:
        copy.wait()


def finish(blocks, near_lists, *args):
    total, n = args[0].shape
    return pl.pallas_call(
        functools.partial(out_kernel, blocks),
        out_shape=jax.ShapeDtypeStruct((total, n), f32),
        in_specs=[SMEM] + [VMEM] * len(args),
        out_specs=pl.BlockSpec(memory_space=pl.ANY),
        scratch_shapes=[pltpu.VMEM((total, n), f32), pltpu.SemaphoreType.DMA((len(blocks),))],
        compiler_params=params(),
        name="finish",
    )(near_lists, *args)


def shifted(value, by):
    size = lax.axis_size("clus")
    pairs = [(i, i + by) for i in range(size) if 0 <= i + by < size]
    return lax.ppermute(value, "clus", pairs)


def both_ways(value):
    return shifted(value, 1), shifted(value, -1)


def on_device(points, weights, targets, near_lists, tile_counts, skeleton):
    features = points.shape[0]
    size = lax.axis_size("leaf")
    steps = [[(i, i ^ (1 << k)) for i in range(0, size, 1 << k)] for k in range(4)]

    pick, note, kept = prep(near_lists, points, skeleton)
    note_b, note_a = both_ways(note)
    first = jnp.concatenate([points, weights[:EARLY_ROWS]], axis=0)
    before_1, after_1 = both_ways(first)
    to_b, to_a = push(points, weights, note_b, note_a)
    from_b = shifted(to_a, 1)
    from_a = shifted(to_b, -1)
    second = weights[EARLY_ROWS:]
    before_2, after_2 = both_ways(second)
    swaps = [[(i, i ^ (1 << k)) for i in range(size)] for k in range(4)]
    others = [among_leaves(kept, swaps[k]) for k in range(4)]
    mine, a_high, a_low, b_high, b_low = inverses(
        points, weights, targets, pick, note, kept, others
    )

    v0 = join(mine, from_b, from_a)
    base = own_near(points, weights, targets, near_lists)
    tiles = near_tiles(points, before_1, after_1, near_lists)
    shared = (tiles, pick, a_high, a_low, near_lists)
    res_1, sol_1 = near_part(0, EARLY_ROWS, features, base, before_1, after_1, *shared)
    tile, place = tables(points, note, pick)

    v1 = level_step(0, v0, among_leaves(v0, steps[0]), b_high, b_low)
    v2 = level_step(1, v1, among_leaves(v1.astype(bf16), steps[1]), b_high, b_low)
    v3 = level_step(2, v2, among_leaves(v2.astype(bf16), steps[2]), b_high, b_low)
    w4 = among_leaves(v3.astype(bf16), steps[3])
    ready, corr = last_part(
        EARLY_ROWS, base, before_2, after_2, *shared, res_1, sol_1, v1, v2, v3, place
    )
    return finish((192, 192, 128), near_lists, ready, corr, v3, w4, b_high, b_low, tile, place)


def solution(mesh):
    split_cols = P(None, ("clus", "leaf"))
    split_rows = P(("clus", "leaf"), None)
    placed = (split_cols, split_cols, split_cols, split_rows, P(("clus", "leaf")), split_rows)

    return jax.shard_map(
        on_device, mesh=mesh, in_specs=placed, out_specs=split_cols, check_vma=False
    )
```
